32 devices in a mesh: sky: 8 (over z, x), tm: 4 (over y, core).
Axes of the slice: x: 2, y: 2, z: 4, core: 2. Of those that a mesh axis runs over, the one named last changes fastest.
Arguments:
- observed: float32 [4096, 128], P(('sky', 'tm')), may hold values from -12 to 12
- att_partials: bfloat16 [3, 4096, 128], P(None, ('sky', 'tm')), may hold values from -6 to 6
- src_partials: bfloat16 [5, 4096, 128], P(None, ('sky', 'tm')), may hold values from -6 to 6
- src_slot: int32 [4096], P(('sky', 'tm')), may hold values from 0 to 1023
- knot_block: int32 [4096], P(('sky', 'tm')), may hold values from 0 to 255, as said below
- live_count: int32 [32], P(('sky', 'tm')), may hold values from 32 to 128, as said below
- sources: float32 [5, 8192], P(None, 'sky'), may hold values from -6 to 6
- inverses: float32 [5, 5, 8192], P(None, None, 'sky')
- attitude: float32 [3, 4, 4096], P(None, 'tm', 'sky'), may hold values from -6 to 6
- band_coef: float32 [3, 3, 4, 4096], P(None, None, 'tm', 'sky'), may hold values from 0.5 to 4
- extra_diag: float32 [3, 4, 4096], P(None, 'tm', 'sky'), may hold values from 0.05 to 0.5
- band_offsets: int32 [3], replicated, may hold values from 1 to 16, as said below
Outputs:
- sources_out: float32 [5, 8192], P(None, 'sky')
- attitude_out: float32 [3, 4, 4096], P(None, 'tm', 'sky')
The draws below stay inside these ranges and needn't reach their ends.
Inputs may be any that keep to these rules, and one draw needn't show every extreme that they name: On every device, the crossings name blocks of one holder (knot_block // 32) at most 32 times, and some holder exactly 32 times; dead crossings carry blocks too. `live_count`: some device uses all its crossings. `band_offsets`: Distinct; one of them is 16.
All inputs are finite; a program needn't handle non-finite values.
Results may differ from the reference program's by a relative error of at most 0.0003.
Values sent between devices are 32-bit elements; how exact they have to be, the bound alone decides.
A program may use at most 64 MiB of HBM per device.

```python
import math
import jax
import jax.numpy as jnp
from jax import lax

CROSS_DEV = 128
ROWS = 128
BLOCK_KNOTS = 16
SRC_DEV = 1024
NB = 3
HW = 16
SWEEPS = 3
ITERS = 2
BLK_DEV = 32
NBLK = 256
SUBK = 4096
CAP = 32
SOURCES = 8192
CROSSINGS = 4096
N_TM = 4


def draw_knot_block(key, part):
    devices_all = CROSSINGS // CROSS_DEV
    holders = NBLK // BLK_DEV
    slot_total = holders * CAP

    def one_device(device_key):
        key_full, key_score, key_order, key_local = jax.random.split(device_key, 4)
        full_holder = jax.random.randint(key_full, (), 0, holders)
        slot_ids = jnp.arange(slot_total, dtype=jnp.int32)
        scores = jax.random.randint(key_score, (slot_total,), 0, 65536)
        scores = jnp.where(slot_ids // CAP == full_holder, -1, scores)
        ranked = jnp.argsort(scores * slot_total + slot_ids)
        chosen = ranked[:CROSS_DEV] // CAP
        chosen = chosen[jax.random.permutation(key_order, CROSS_DEV)]
        local_blocks = jax.random.randint(key_local, (CROSS_DEV,), 0, BLK_DEV)
        return (chosen * BLK_DEV + local_blocks).astype(jnp.int32)
    keys_all = jax.random.split(jax.random.fold_in(key, 11), devices_all)
    return jax.vmap(one_device)(keys_all).reshape(-1)


def draw_live_count(key, part):
    devices_all = CROSSINGS // CROSS_DEV
    key_div, key_full = jax.random.split(jax.random.fold_in(key, 23))
    divisor = jax.random.randint(key_div, (devices_all,), 1, 5)
    counts = CROSS_DEV // divisor
    full_device = jax.random.randint(key_full, (), 0, devices_all)
    return counts.at[full_device].set(CROSS_DEV).astype(jnp.int32)


def draw_band_offsets(key, part):
    key_pick, key_place = jax.random.split(jax.random.fold_in(key, 37))
    order = jax.random.permutation(key_pick, HW - 1) + 1
    picked = jnp.concatenate([jnp.full((1,), HW, jnp.int32), order[:NB - 1].astype(jnp.int32)])
    placed = jax.random.permutation(key_place, NB)
    return picked[placed].astype(jnp.int32)


def draw_inverses(key, part):
    key_scale, key_noise = jax.random.split(jax.random.fold_in(key, 51))
    scales = jnp.exp(jax.random.uniform(key_scale, (5, SOURCES), jnp.float32, jnp.log(0.001), jnp.log(0.012)))
    noise = 0.2 * jax.random.normal(key_noise, (5, 5, SOURCES), jnp.float32)
    symmetric = 0.5 * (noise + jnp.transpose(noise, (1, 0, 2)))
    identity = jnp.eye(5, dtype=jnp.float32)
    shape_part = identity[:, :, None] + symmetric * (1.0 - identity)[:, :, None]
    return (shape_part * jnp.sqrt(scales[:, None, :] * scales[None, :, :])).astype(jnp.float32)


def place_ends(array, stream_key, low, top_value):
    spot = [jax.random.randint(jax.random.fold_in(stream_key, axis), (), 0, length) for axis, length in enumerate(array.shape)]
    main_axis = array.shape.index(max(array.shape))
    next_to = spot[:main_axis] + [(spot[main_axis] + 1) % array.shape[main_axis]] + spot[main_axis + 1:]
    return array.at[tuple(spot)].set(low).at[tuple(next_to)].set(top_value)


def block_scale(rng, extent, cuts, low, top_value):
    def one(axis_at, blocks):
        heights = jax.random.uniform(jax.random.fold_in(jax.random.fold_in(rng, 6), axis_at), (blocks,), jnp.float32, low / len(cuts), top_value / len(cuts))
        return jnp.repeat(jnp.exp(heights), extent[axis_at] // blocks).reshape((-1,) + (1,) * (len(extent) - axis_at - 1))

    gain = one(*cuts[0])
    for cut in cuts[1:]:
        gain = gain * one(*cut)
    return gain


def bell_draw(rng, shape, deviation, limit, cuts=(), kind=jnp.bfloat16):
    array = deviation * jax.random.normal(rng, shape, jnp.float32)
    if cuts:
        array = array * block_scale(rng, shape, cuts, -0.22, 0.18)
    return jnp.clip(array, -limit, limit).astype(kind)


def setup_inputs(seed: int = 0) -> dict:
    keys = jax.random.split(jax.random.key(seed), 13)
    observed = bell_draw(keys[0], (CROSSINGS, ROWS), 2.0, 12.0, ((0, 32),), jnp.float32)
    att_partials = bell_draw(keys[1], (3, CROSSINGS, ROWS), 1.0, 6.0, ((1, 32),))
    src_partials = bell_draw(keys[2], (5, CROSSINGS, ROWS), 1.0, 6.0, ((1, 32),))
    src_slot = place_ends(jax.random.randint(keys[3], (CROSSINGS,), 0, SRC_DEV), jax.random.fold_in(keys[3], 1), 0, SRC_DEV - 1).astype(jnp.int32)
    knot_block = draw_knot_block(jax.random.fold_in(keys[12], 71), 0)
    live_count = draw_live_count(jax.random.fold_in(keys[12], 71), 0)
    sources = bell_draw(keys[6], (5, SOURCES), 1.0, 6.0, ((1, 8),), jnp.float32)
    inverses = draw_inverses(jax.random.fold_in(keys[12], 71), 0)
    attitude = bell_draw(keys[8], (3, N_TM, SUBK), 1.0, 6.0, ((1, 4), (2, 8)), jnp.float32)
    band_coef = jnp.clip(jnp.exp(math.log(4.0) - 2.0794415 * jax.random.uniform(keys[9], (NB, 3, N_TM, SUBK), jnp.float32) ** block_scale(keys[9], (NB, 3, N_TM, SUBK), ((2, 4), (3, 8)), -0.2, 0.2)), 0.5, 4.0)
    extra_diag = jnp.clip(jnp.exp(math.log(0.5) - 2.3025851 * jax.random.uniform(keys[10], (3, N_TM, SUBK), jnp.float32) ** block_scale(keys[10], (3, N_TM, SUBK), ((1, 4), (2, 8)), -0.2, 0.2)), 0.05, 0.5)
    band_offsets = draw_band_offsets(jax.random.fold_in(keys[12], 71), 0)
    return dict(observed=observed, att_partials=att_partials, src_partials=src_partials, src_slot=src_slot, knot_block=knot_block, live_count=live_count, sources=sources, inverses=inverses, attitude=attitude, band_coef=band_coef, extra_diag=extra_diag, band_offsets=band_offsets)


def spline_table():
    rows_pos = jnp.arange(ROWS, dtype=jnp.float32)
    moments = 1.5 + (BLOCK_KNOTS - 3) * (rows_pos + 0.5) / ROWS
    knot_pos = jnp.arange(BLOCK_KNOTS, dtype=jnp.float32)
    dist = jnp.abs(moments[:, None] - knot_pos[None, :])
    inner = 2.0 / 3.0 - dist * dist + 0.5 * dist * dist * dist
    rest = 2.0 - dist
    outer = rest * rest * rest / 6.0
    return jnp.where(dist < 1.0, inner, jnp.where(dist < 2.0, outer, 0.0))


def source_term(src_partials, values):
    total = jnp.zeros(src_partials.shape[1:], jnp.float32)
    for component in range(5):
        total = total + src_partials[component].astype(jnp.float32) * values[component][:, None]
    return total


def neighbour_sum(field, band_terms, band_offsets, base, length):
    total = jnp.zeros(band_terms.shape[1:], jnp.float32)
    for band_index in range(band_terms.shape[0]):
        offset = band_offsets[band_index].astype(jnp.int32)
        upper = lax.dynamic_slice_in_dim(field, base + offset, length, 1)
        lower = lax.dynamic_slice_in_dim(field, base - offset, length, 1)
        total = total + band_terms[band_index] * (upper + lower)
    return total


def reference(observed, att_partials, src_partials, src_slot, knot_block, live_count, sources, inverses, attitude, band_coef, extra_diag, band_offsets):
    spline = spline_table()
    crossing_count = observed.shape[0]
    position = jnp.arange(crossing_count, dtype=jnp.int32)
    device = position // CROSS_DEV
    sky_block = device // N_TM
    interval = device % N_TM
    live_rows = ((position % CROSS_DEV) < live_count[device]).astype(jnp.float32)[:, None]
    source_index = sky_block * SRC_DEV + src_slot
    block_index = interval * NBLK + knot_block
    knot_total = N_TM * SUBK
    band_terms = band_coef.reshape(NB, 3, knot_total)
    diagonal = extra_diag.reshape(3, knot_total) + 2.0 * jnp.sum(band_terms, axis=0)
    sources_now = sources
    knots_now = attitude.reshape(3, knot_total)
    for outer_step in range(ITERS):
        fetched = jnp.take(knots_now.reshape(3, N_TM * NBLK, BLOCK_KNOTS), block_index, axis=1)
        att_term = jnp.zeros(observed.shape, jnp.float32)
        for axis_index in range(3):
            att_term = att_term + att_partials[axis_index].astype(jnp.float32) * jnp.dot(fetched[axis_index], spline.T, precision=lax.Precision.HIGHEST)
        src_values = jnp.take(sources_now, source_index, axis=1)
        resid = (observed - source_term(src_partials, src_values) - att_term) * live_rows
        rhs = jnp.stack([jnp.sum(src_partials[component].astype(jnp.float32) * resid, axis=1) for component in range(5)])
        normal = jax.ops.segment_sum(rhs.T, source_index, num_segments=SOURCES).T
        step = jnp.einsum("klm,lm->km", inverses, normal, precision=lax.Precision.HIGHEST)
        sources_now = sources_now + step
        resid = resid - live_rows * source_term(src_partials, jnp.take(step, source_index, axis=1))
        grads = jnp.stack([jnp.dot(att_partials[axis_index].astype(jnp.float32) * resid, spline, precision=lax.Precision.HIGHEST) for axis_index in range(3)])
        knot_grad = jnp.stack([jax.ops.segment_sum(grads[axis_index], block_index, num_segments=N_TM * NBLK) for axis_index in range(3)]).reshape(3, knot_total)
        delta = knot_grad / diagonal
        for sweep_index in range(SWEEPS - 1):
            padded = jnp.pad(delta, ((0, 0), (HW, HW)))
            delta = (knot_grad + neighbour_sum(padded, band_terms, band_offsets, HW, knot_total)) / diagonal
        knots_now = knots_now + delta
    return sources_now, knots_now.reshape(3, N_TM, SUBK)
```

```python
import functools

import jax
import jax.numpy as jnp
from jax import lax
from jax.experimental import pallas as pl
from jax.experimental.pallas import tpu as pltpu
from jax.sharding import PartitionSpec as P

BLOCK_KNOTS = 16
SWEEPS = 3
ITERS = 2
NPAR = 5
NAX = 3
LANES = 128
REACH = 2
HOT_CAP = 4 << 20
MESH = pl.DeviceIdType.MESH
F32 = jnp.float32
BF16 = jnp.bfloat16

NN = (((1,), (0,)), ((), ()))
NT = (((1,), (1,)), ((), ()))


def iota(shape, dim):
    return lax.broadcasted_iota(jnp.int32, shape, dim)


def onehot(mask):
    return jnp.where(mask, 1.0, 0.0).astype(BF16)


def parts(x):
    high = x.astype(BF16)
    return high, (x - high.astype(F32)).astype(BF16)


def mm(a, b, dims=NN):
    return lax.dot_general(a, b, dims, preferred_element_type=F32)


def left_dot(x, hot, dims=NN):
    n = x.shape[0]
    out = mm(jnp.concatenate(parts(x), axis=0), hot, dims)
    return out[:n] + out[n:]


def spline_at(row, knot, rows):
    moment = 1.5 + (BLOCK_KNOTS - 3) * (row.astype(F32) + 0.5) / rows
    dist = jnp.abs(moment - knot.astype(F32))
    inner = 2.0 / 3.0 - dist * dist + 0.5 * dist * dist * dist
    rest = 2.0 - dist
    outer = rest * rest * rest / 6.0
    return jnp.where(dist < 1.0, inner, jnp.where(dist < 2.0, outer, 0.0))


def partner(me, i, n):
    if n & (n - 1):
        return lax.rem(me + i, n)
    out, bit = me, 1
    while bit < n:
        out = out + ((i // bit) % 2) * bit * (1 - 2 * ((me // bit) % 2))
        bit *= 2
    return out


def kernel(
    n_sky,
    n_tm,
    observed,
    att_partials,
    src_partials,
    src_slot,
    knot_block,
    live_count,
    sources,
    inverses,
    attitude,
    band_coef,
    extra_diag,
    band_offsets,
    sources_out,
    attitude_out,
    knots_all,
    coef_all,
    kb_all,
    slots_all,
    rhs_all,
    grads_all,
    rim_mine,
    rim_all,
    win_mine,
    win_all,
    win_low,
    win_high,
    coef_win,
    moved_all,
    hot_all,
    knots_send,
    knots_recv,
    coef_send,
    coef_recv,
    kb_send,
    kb_recv,
    near_send,
    near_recv,
    pass_send,
    pass_recv,
    slots_send,
    slots_recv,
    rhs_send,
    rhs_recv,
    grads_send,
    grads_recv,
    rim_send,
    rim_recv,
    win_send,
    win_recv,
    far_send,
    low_recv,
    high_recv,
):
    s = lax.axis_index("sky")
    t = lax.axis_index("tm")
    cross, rows = observed.shape
    knots_here = attitude.shape[2]
    blocks = knots_here // BLOCK_KNOTS
    span = blocks + 2 * REACH
    n_blocks = n_sky * blocks
    n_src = sources.shape[1]
    n_band = band_coef.shape[0]
    tile = moved_all.shape[2]
    wide = n_sky * tile
    n_coef = (1 + n_band) * BLOCK_KNOTS
    k16 = BLOCK_KNOTS

    first_t, last_t = t == 0, t == n_tm - 1
    at_low, at_high = s == 0, s == n_sky - 1
    not_first, not_last = t > 0, t < n_tm - 1
    t_up, t_down = jnp.minimum(t + 1, n_tm - 1), jnp.maximum(t - 1, 0)

    barrier = pltpu.get_barrier_semaphore()
    for i in range(n_sky - 1, 0, -1):
        pl.semaphore_signal(barrier, inc=1, device_id=(partner(s, i, n_sky), t), device_id_type=MESH)
    for i in range(n_tm - 1, 0, -1):
        pl.semaphore_signal(barrier, inc=1, device_id=(s, partner(t, i, n_tm)), device_id_type=MESH)

    def remote(src, dst, send, recv, to):
        return pltpu.make_async_remote_copy(
            src_ref=src, dst_ref=dst, send_sem=send, recv_sem=recv, device_id=to, device_id_type=MESH
        )

    def to_sky(i):
        return (partner(s, i, n_sky), t)

    def to_tm(i):
        return (s, partner(t, i, n_tm))

    def knots_copy(i):
        return remote(knots_all.at[s], knots_all.at[s], knots_send.at[i], knots_recv.at[i], to_sky(i))

    def coef_copy(i):
        return remote(coef_all.at[s], coef_all.at[s], coef_send.at[i], coef_recv.at[i], to_sky(i))

    def kb_copy(i):
        return remote(kb_all.at[s], kb_all.at[s], kb_send.at[i], kb_recv.at[i], to_sky(i))

    def near_copy(side):
        to = (s, t_up if side == 0 else t_down)
        return remote(coef_all.at[s], coef_all.at[n_sky + side], near_send.at[side], near_recv.at[side], to)

    def pass_copy(side, i):
        at = n_sky + side
        return remote(coef_all.at[at], coef_all.at[at], pass_send.at[side, i], pass_recv.at[side], to_sky(i))

    def slots_copy(i):
        return remote(slots_all.at[t], slots_all.at[t], slots_send.at[i], slots_recv.at[i], to_tm(i))

    def rhs_copy(it, i):
        return remote(rhs_all.at[it, t], rhs_all.at[it, t], rhs_send.at[it, i], rhs_recv.at[it, i], to_tm(i))

    def grads_copy(i):
        return remote(grads_all.at[s], grads_all.at[s], grads_send.at[i], grads_recv.at[i], to_sky(i))

    def rim_copy(side, to_s, slot):
        to = (to_s, t_down if side == 0 else t_up)
        return remote(rim_mine.at[side], rim_all.at[side, slot], rim_send.at[side, to_s], rim_recv.at[side, slot], to)

    def win_copy(i):
        to = to_sky(i)
        return remote(win_mine.at[1 + to[0]], win_all.at[s], win_send.at[i], win_recv.at[i], to)

    def low_copy(slot):
        return remote(win_mine.at[n_sky + 1], win_low.at[slot], far_send.at[0], low_recv.at[slot], (0, t_up))

    def high_copy(slot):
        return remote(win_mine.at[0], win_high.at[slot], far_send.at[1], high_recv.at[slot], (n_sky - 1, t_down))

    shape = (knots_here, tile)
    fold = jnp.concatenate(
        [onehot(iota(shape, 1) == (iota(shape, 0) // k16) + (span * a + REACH)) for a in range(NAX)], axis=0
    )
    own_knot = iota((k16, knots_here), 0) == iota((k16, knots_here), 1) % k16

    def to_tile(lines):
        return left_dot(
            jnp.concatenate([jnp.where(own_knot, line, 0.0) for line in lines], axis=1), fold
        )

    knots_all[s] = to_tile([attitude[a] for a in range(NAX)])
    slot_row = src_slot[...].astype(F32)
    block_row = knot_block[...].astype(F32)
    slots_all[t] = slot_row
    bands = [[band_coef[b, a] for a in range(NAX)] for b in range(n_band)]
    inv_diag = []
    for a in range(NAX):
        band_sum = bands[0][a]
        for b in range(1, n_band):
            band_sum = band_sum + bands[b][a]
        inv_diag.append(1.0 / (extra_diag[a] + 2.0 * band_sum))
    coef_all[s, :k16] = to_tile(inv_diag)
    for b in range(n_band):
        coef_all[s, (b + 1) * k16 : (b + 2) * k16] = to_tile([bands[b][a] * inv_diag[a] for a in range(NAX)])
    kb_all[s] = block_row

    pl.semaphore_wait(barrier, (n_sky - 1) + (n_tm - 1))
    for i in range(n_sky - 1, 0, -1):
        knots_copy(i).start()
    for i in range(n_tm - 1, 0, -1):
        slots_copy(i).start()
    take_low, take_high = jnp.logical_and(at_high, not_first), jnp.logical_and(at_low, not_last)

    @pl.when(jnp.logical_and(at_high, not_last))
    def _():
        near_copy(0).start()

    @pl.when(jnp.logical_and(at_low, not_first))
    def _():
        near_copy(1).start()

    for i in range(n_sky - 1, 0, -1):
        kb_copy(i).start()
    for i in range(n_sky - 1, 0, -1):
        coef_copy(i).start()

    lane = iota((1, cross), 1)
    live = lane < live_count[0]

    shape = (n_src, cross)
    src_hot = onehot(iota(shape, 0).astype(F32) == slot_row)
    gap_rows = jnp.zeros((8 - NPAR, n_src), F32)
    src_list = [x for q in range(NPAR) for x in (inverses[q], gap_rows)]
    gathered = left_dot(jnp.concatenate(src_list + [sources[...], gap_rows], axis=0), src_hot)

    eye = onehot(iota((rows, rows), 0) == iota((rows, rows), 1))
    par = [mm(eye, src_partials[p], NT) for p in range(NPAR)]
    att = [mm(eye, att_partials[a], NT) for a in range(NAX)]

    def source_term(values):
        total = par[0] * values[0:1]
        for p in range(1, NPAR):
            total = total + par[p] * values[p : p + 1]
        return total

    base = jnp.transpose(observed[...]) - source_term(gathered[NPAR * 8 :])

    shape = (k16, 2 * rows)
    high, low = parts(spline_at(iota(shape, 1) % rows, iota(shape, 0), rows))
    low = jnp.where(iota(shape, 1) < rows, low.astype(F32), 0.0).astype(BF16)
    back = jnp.concatenate([high, low], axis=0)
    shape = (rows, 3 * k16)
    high, low = parts(spline_at(iota(shape, 0), iota(shape, 1) % k16, rows))
    look = jnp.where(iota(shape, 1) < 2 * k16, high.astype(F32), low.astype(F32)).astype(BF16)

    def back_dot(value):
        spread = jnp.concatenate([x * value for x in att], axis=1)
        out = mm(back, jnp.concatenate(parts(spread), axis=0))
        return out[:k16] + out[k16:]

    def look_dot(knots):
        high, low = parts(knots)
        return mm(look, jnp.concatenate([high, low, high], axis=0))

    cross_terms = [back_dot(par[q]) for q in range(NPAR)]

    def against_params(value):
        return jnp.concatenate(
            [jnp.sum(par[p] * value, axis=0, keepdims=True) for p in range(NPAR)]
            + [jnp.zeros((8 - NPAR, cross), F32)],
            axis=0,
        )

    on_base = against_params(base)

    def targets(shape, first):
        m = iota(shape, 0) + first * tile
        h, at = m // tile - 2, m % tile
        i = at
        for a in range(1, NAX):
            i = i - jnp.where(at >= a * span, span, 0)
        found = h * blocks - REACH + i
        return jnp.where(at >= NAX * span, -1, found), i

    shape = (wide, cross)
    target, place = targets(shape, 2)
    inside = jnp.logical_and(place >= REACH, place < REACH + blocks)
    knot_hot = onehot(jnp.where(inside, target, -1).astype(F32) == block_row)

    at_lane = iota((k16, wide), 1) % tile
    axis_masks = [
        jnp.logical_and(at_lane >= a * span, at_lane < (a + 1) * span) for a in range(NAX)
    ]

    def fetch(tiles):
        masked = jnp.concatenate([jnp.where(mask, tiles, 0.0) for mask in axis_masks], axis=0)
        got = left_dot(masked, knot_hot)
        return jnp.concatenate([got[a * k16 : (a + 1) * k16] for a in range(NAX)], axis=1)

    for i in range(1, n_tm):
        slots_copy(i).wait_recv()
    slots_row = jnp.concatenate([slots_all[i] for i in range(n_tm)], axis=1)
    slot_col = jnp.transpose(jnp.broadcast_to(slot_row, (LANES, cross)))[:, :1]
    same_source = onehot(slot_col == slots_row)

    @pl.when(take_low)
    def _():
        near_copy(0).wait_recv()
        for i in range(n_sky - 1, 0, -1):
            pass_copy(0, i).start()

    @pl.when(take_high)
    def _():
        near_copy(1).wait_recv()
        for i in range(n_sky - 1, 0, -1):
            pass_copy(1, i).start()

    shape = (n_band * k16, 3 * k16)
    c, d = iota(shape, 0), iota(shape, 1)
    gap = jnp.abs(d - k16 - c % k16)
    offset = jnp.zeros(shape, jnp.int32)
    for b in range(n_band):
        offset = jnp.where(c // k16 == b, band_offsets[b], offset)
    shift_hot = onehot(gap == offset)
    shift_hot = jnp.concatenate([shift_hot, shift_hot], axis=1)

    def smooth(grad, inv, terms):
        first = grad * inv
        delta = first
        for sweep in range(SWEEPS - 1):
            n = delta.shape[1] // tile
            cut = [delta[:, h * tile : (h + 1) * tile] for h in range(n)]
            before = jnp.concatenate([pltpu.roll(x, 1, 1) for x in cut], axis=1)
            after = jnp.concatenate([pltpu.roll(x, tile - 1, 1) for x in cut], axis=1)
            near = jnp.concatenate([before, delta, after], axis=0)
            sums = mm(shift_hot, jnp.concatenate(parts(near), axis=0))
            delta = first
            for b in range(n_band):
                delta = delta + terms[b] * sums[b * k16 : (b + 1) * k16]
        return delta

    for i in range(1, n_sky):
        knots_copy(i).wait_recv()
    fetched = fetch(jnp.concatenate([knots_all[h] for h in range(n_sky)], axis=1))

    def send_rhs(it, fetched, on_base):
        out = []
        for q in range(NPAR):
            term = jnp.sum(fetched * cross_terms[q], axis=0, keepdims=True)
            total = term[:, :cross]
            for a in range(1, NAX):
                total = total + term[:, a * cross : (a + 1) * cross]
            out.append(total)
        out.append(jnp.zeros((8 - NPAR, cross), F32))
        rhs_all[it, t] = jnp.where(live, on_base - jnp.concatenate(out, axis=0), 0.0)
        for i in range(n_tm - 1, 0, -1):
            rhs_copy(it, i).start()

    def grads_of(base, fetched):
        seen = look_dot(fetched)
        resid = base
        for a in range(NAX):
            resid = resid - att[a] * seen[:, a * cross : (a + 1) * cross]
        return back_dot(jnp.where(live, resid, 0.0))

    def wait_rhs(it):
        for i in range(1, n_tm):
            rhs_copy(it, i).wait_recv()
        return jnp.concatenate([rhs_all[it, i] for i in range(n_tm)], axis=1)

    live_all = jnp.concatenate([live] * NAX, axis=1)

    def step_of(rhs):
        normal = left_dot(rhs, same_source, NT)
        return [
            jnp.sum(gathered[q * 8 : (q + 1) * 8] * normal, axis=0, keepdims=True)
            for q in range(NPAR)
        ]

    def move_grads(grads, step):
        total = jnp.concatenate([step[0]] * NAX, axis=1) * cross_terms[0]
        for q in range(1, NPAR):
            total = total + jnp.concatenate([step[q]] * NAX, axis=1) * cross_terms[q]
        return grads - jnp.where(live_all, total, 0.0)

    send_rhs(0, fetched, on_base)
    grads = grads_of(base, fetched)

    for i in range(1, n_sky):
        kb_copy(i).wait_recv()

    prebuilt = hot_all.shape[0] == n_sky

    def sender_hot(h):
        return onehot(target.astype(F32) == kb_all[h])

    if prebuilt:
        @pl.loop(0, n_sky)
        def _(h):
            hot_all[h] = sender_hot(h)

    rim_row = iota((k16, cross), 0)
    rim_block = jnp.where(rim_row < 8, rim_row, n_blocks - REACH - 8 + rim_row)
    rim_hot = onehot(
        jnp.logical_and(rim_row % 8 < REACH, rim_block.astype(F32) == block_row)
    )

    rhs = wait_rhs(0)
    rhs_total = rhs
    step = step_of(rhs)
    grads = move_grads(grads, step)
    grads_all[s] = grads
    for i in range(n_sky - 1, 0, -1):
        grads_copy(i).start()

    high, low = parts(jnp.concatenate([grads[:, a * cross : (a + 1) * cross] for a in range(NAX)], axis=0))
    gap_rows = jnp.zeros((LANES - NAX * k16, cross), BF16)
    rims = mm(rim_hot, jnp.concatenate([high, gap_rows], axis=0), NT) + mm(
        rim_hot, jnp.concatenate([low, gap_rows], axis=0), NT
    )
    rim_mine[0] = rims[:REACH]
    rim_mine[1] = rims[8 : 8 + REACH]

    @pl.when(not_first)
    def _():
        for i in range(n_sky - 1, -1, -1):
            rim_copy(0, partner(s, i, n_sky), s).start()

    @pl.when(not_last)
    def _():
        for i in range(n_sky - 1, -1, -1):
            rim_copy(1, partner(s, i, n_sky), s).start()

    base = base - source_term(jnp.concatenate(step, axis=0))
    on_base = against_params(base)
    for i in range(1, n_sky):
        coef_copy(i).wait_recv()

    @pl.when(jnp.logical_and(not_first, jnp.logical_not(at_high)))
    def _():
        pass_copy(0, 1).wait_recv()

    @pl.when(jnp.logical_and(not_last, jnp.logical_not(at_low)))
    def _():
        pass_copy(1, 1).wait_recv()

    @pl.when(first_t)
    def _():
        coef_all[n_sky] = jnp.zeros(coef_all.shape[1:], F32)
        rim_all[1] = jnp.zeros(rim_all.shape[1:], F32)

    @pl.when(last_t)
    def _():
        coef_all[n_sky + 1] = jnp.zeros(coef_all.shape[1:], F32)
        rim_all[0] = jnp.zeros(rim_all.shape[1:], F32)

    at = iota((n_coef, tile), 1)
    is_low, is_high = at < 0, at < 0
    for a in range(NAX):
        begin = a * span
        is_low = jnp.logical_or(is_low, jnp.logical_and(at >= begin, at < begin + REACH))
        begin = a * span + REACH + blocks
        is_high = jnp.logical_or(is_high, jnp.logical_and(at >= begin, at < begin + REACH))
    for h in range(n_sky):
        low_at = h - 1 if h > 0 else n_sky
        high_at = h + 1 if h < n_sky - 1 else n_sky + 1
        low = pltpu.roll(coef_all[low_at], tile - blocks, 1)
        high = pltpu.roll(coef_all[high_at], blocks, 1)
        coef_win[h] = jnp.where(is_low, low, jnp.where(is_high, high, coef_all[h]))

    def coef_wide(b):
        return jnp.concatenate([coef_win[h, b * k16 : (b + 1) * k16] for h in range(n_sky)], axis=1)

    inv_wide = coef_wide(0)
    terms_wide = [coef_wide(b + 1) for b in range(n_band)]

    shape = (2 * REACH * LANES, 2 * tile)
    c, d = iota(shape, 0), iota(shape, 1)
    r, c = c // LANES, c % LANES
    spot = (c // k16) * span + jnp.where(r < REACH, r, tile + blocks + r)
    rim_fold = onehot(jnp.logical_and(c < NAX * k16, d == spot))
    rim_knot = iota((k16, LANES), 0) == iota((k16, LANES), 1) % k16

    @pl.when(not_last)
    def _():
        for i in range(n_sky):
            rim_copy(0, i, i).wait_recv()

    @pl.when(not_first)
    def _():
        for i in range(n_sky):
            rim_copy(1, i, i).wait_recv()

    rim_rows = []
    for side in (1, 0):
        total = rim_all[side, 0]
        for i in range(1, n_sky):
            total = total + rim_all[side, i]
        rim_rows = rim_rows + [total[i : i + 1] for i in range(REACH)]
    rim_tiles = left_dot(
        jnp.concatenate([jnp.where(rim_knot, row, 0.0) for row in rim_rows], axis=1), rim_fold
    )

    group = 2 if n_sky % 2 == 0 else 1

    def scatter(j, total):
        home = partner(s // group, j, n_sky // group) * group
        got = [grads_all[home + x] for x in range(group)]
        hots = [hot_all[home + x] if prebuilt else sender_hot(home + x) for x in range(group)]
        lines = [
            jnp.concatenate([g[:, a * cross : (a + 1) * cross] for g in got], axis=1)
            for a in range(NAX)
        ]
        out = left_dot(jnp.concatenate(lines, axis=0), jnp.concatenate(hots, axis=1), NT)
        picked = out[(NAX - 1) * k16 :]
        for a in range(NAX - 2, -1, -1):
            picked = jnp.where(at_lane < (a + 1) * span, out[a * k16 : (a + 1) * k16], picked)
        return total + picked

    for x in range(1, group):
        grads_copy(x).wait_recv()
    grad = scatter(0, jnp.zeros((k16, wide), F32))

    def add_group(j, total):
        for x in range(group):
            grads_copy(j * group + x).wait_recv()
        return scatter(j, total)

    if prebuilt:
        for j in range(1, n_sky // group):
            grad = add_group(j, grad)
    else:
        grad = lax.fori_loop(1, n_sky // group, add_group, grad)

    grad = jnp.concatenate(
        [grad[:, :tile] + rim_tiles[:, :tile], grad[:, tile : wide - tile], grad[:, wide - tile :] + rim_tiles[:, tile:]],
        axis=1,
    )
    delta = smooth(grad, inv_wide, terms_wide)
    for h in range(n_sky):
        moved_all[h] = delta[:, h * tile : (h + 1) * tile]
    fetched = fetched + fetch(delta)
    send_rhs(1, fetched, on_base)
    grads = grads_of(base, fetched)
    target_own, _ = targets(((n_sky + 2) * tile, cross), 1)
    win_hot = onehot(target_own.astype(F32) == block_row)
    rhs = wait_rhs(1)
    rhs_total = rhs_total + rhs
    grads = move_grads(grads, step_of(rhs))
    lines = jnp.concatenate([grads[:, a * cross : (a + 1) * cross] for a in range(NAX)], axis=0)
    out = left_dot(lines, win_hot, NT)
    at_lane = iota((k16, (n_sky + 2) * tile), 1) % tile
    picked = out[(NAX - 1) * k16 :]
    for a in range(NAX - 2, -1, -1):
        picked = jnp.where(at_lane < (a + 1) * span, out[a * k16 : (a + 1) * k16], picked)
    for h in range(n_sky + 2):
        win_mine[h] = picked[:, h * tile : (h + 1) * tile]

    for i in range(n_sky - 1, 0, -1):
        win_copy(i).start()

    @pl.when(not_last)
    def _():
        low_copy(s).start()

    @pl.when(not_first)
    def _():
        high_copy(s).start()

    win_all[s] = win_mine[1 + s]
    from_low, from_high = jnp.logical_and(at_low, not_first), jnp.logical_and(at_high, not_last)

    @pl.when(jnp.logical_not(from_low))
    def _():
        win_low[...] = jnp.zeros(win_low.shape, F32)

    @pl.when(jnp.logical_not(from_high))
    def _():
        win_high[...] = jnp.zeros(win_high.shape, F32)

    full_hot = onehot(iota((n_src, n_tm * cross), 0).astype(F32) == slots_row)
    normal_all = left_dot(rhs_total, full_hot, NT)[:NPAR]
    steps = [jnp.sum(inverses[q] * normal_all, axis=0, keepdims=True) for q in range(NPAR)]
    sources_out[...] = sources[...] + jnp.concatenate(steps, axis=0)
    inv_own = coef_win[s, :k16]
    terms_own = [coef_win[s, (b + 1) * k16 : (b + 2) * k16] for b in range(n_band)]

    for i in range(1, n_sky):
        win_copy(i).wait_recv()

    @pl.when(from_low)
    def _():
        for i in range(n_sky):
            low_copy(i).wait_recv()

    @pl.when(from_high)
    def _():
        for i in range(n_sky):
            high_copy(i).wait_recv()

    grad = win_all[0] + win_low[0] + win_high[0]
    for i in range(1, n_sky):
        grad = grad + (win_all[i] + win_low[i] + win_high[i])
    moved = moved_all[s] + smooth(grad, inv_own, terms_own)

    line = left_dot(moved, fold, NT)
    for a in range(NAX):
        own = jnp.where(own_knot, line[:, a * knots_here : (a + 1) * knots_here], 0.0)
        attitude_out[a] = attitude[a] + jnp.sum(own, axis=0, keepdims=True)

    for i in range(1, n_sky):
        knots_copy(i).wait_send()
        coef_copy(i).wait_send()
        kb_copy(i).wait_send()
        grads_copy(i).wait_send()
        win_copy(i).wait_send()
    for i in range(1, n_tm):
        slots_copy(i).wait_send()
        for it in range(ITERS):
            rhs_copy(it, i).wait_send()

    @pl.when(jnp.logical_and(at_high, not_last))
    def _():
        near_copy(0).wait_send()

    @pl.when(jnp.logical_and(at_low, not_first))
    def _():
        near_copy(1).wait_send()

    @pl.when(take_low)
    def _():
        for i in range(1, n_sky):
            pass_copy(0, i).wait_send()

    @pl.when(take_high)
    def _():
        for i in range(1, n_sky):
            pass_copy(1, i).wait_send()

    @pl.when(not_first)
    def _():
        for i in range(n_sky):
            rim_copy(0, i, s).wait_send()
        high_copy(s).wait_send()

    @pl.when(not_last)
    def _():
        for i in range(n_sky):
            rim_copy(1, i, s).wait_send()
        low_copy(s).wait_send()


def finish(sources_in, attitude_in, sources_out, attitude_out):
    sources_out[...] = sources_in[...]
    attitude_out[...] = attitude_in[...]


def per_device(
    observed,
    att_partials,
    src_partials,
    src_slot,
    knot_block,
    live_count,
    sources,
    inverses,
    attitude,
    band_coef,
    extra_diag,
    band_offsets,
):
    n_sky, n_tm = lax.axis_size("sky"), lax.axis_size("tm")
    blocks = attitude.shape[2] // BLOCK_KNOTS
    cross = src_slot.shape[0]
    k16 = BLOCK_KNOTS
    tile = -(-NAX * (blocks + 2 * REACH) // LANES) * LANES
    n_coef = (1 + band_coef.shape[0]) * k16
    n_hot = n_sky if n_sky * n_sky * tile * cross * 2 <= HOT_CAP else 1
    vmem = pl.BlockSpec(memory_space=pltpu.VMEM)
    smem = pl.BlockSpec(memory_space=pltpu.SMEM)
    dma = pltpu.SemaphoreType.DMA
    results = pl.pallas_call(
        functools.partial(kernel, n_sky, n_tm),
        out_shape=(
            jax.ShapeDtypeStruct(sources.shape, F32),
            jax.ShapeDtypeStruct(attitude.shape, F32),
        ),
        in_specs=[vmem] * 5 + [smem] + [vmem] * 5 + [smem],
        out_specs=(vmem, vmem),
        scratch_shapes=[
            pltpu.VMEM((n_sky, k16, tile), F32),
            pltpu.VMEM((n_sky + 2, n_coef, tile), F32),
            pltpu.VMEM((n_sky, 1, cross), F32),
            pltpu.VMEM((n_tm, 1, cross), F32),
            pltpu.VMEM((ITERS, n_tm, 8, cross), F32),
            pltpu.VMEM((n_sky, k16, NAX * cross), F32),
            pltpu.VMEM((2, REACH, LANES), F32),
            pltpu.VMEM((2, n_sky, REACH, LANES), F32),
            pltpu.VMEM((n_sky + 2, k16, tile), F32),
            pltpu.VMEM((n_sky, k16, tile), F32),
            pltpu.VMEM((n_sky, k16, tile), F32),
            pltpu.VMEM((n_sky, k16, tile), F32),
            pltpu.VMEM((n_sky, n_coef, tile), F32),
            pltpu.VMEM((n_sky, k16, tile), F32),
            pltpu.VMEM((n_hot, n_sky * tile, cross), BF16),
            dma((n_sky,)),
            dma((n_sky,)),
            dma((n_sky,)),
            dma((n_sky,)),
            dma((n_sky,)),
            dma((n_sky,)),
            dma((2,)),
            dma((2,)),
            dma((2, n_sky)),
            dma((2,)),
            dma((n_tm,)),
            dma((n_tm,)),
            dma((ITERS, n_tm)),
            dma((ITERS, n_tm)),
            dma((n_sky,)),
            dma((n_sky,)),
            dma((2, n_sky)),
            dma((2, n_sky)),
            dma((n_sky,)),
            dma((n_sky,)),
            dma((2,)),
            dma((n_sky,)),
            dma((n_sky,)),
        ],
        compiler_params=pltpu.CompilerParams(
            collective_id=0, has_side_effects=True
        ),
    )(
        observed,
        att_partials,
        src_partials,
        src_slot[None, :],
        knot_block[None, :],
        live_count,
        sources,
        inverses,
        attitude,
        band_coef,
        extra_diag,
        band_offsets,
    )
    return pl.pallas_call(
        finish,
        out_shape=(
            jax.ShapeDtypeStruct(sources.shape, F32),
            jax.ShapeDtypeStruct(attitude.shape, F32),
        ),
        in_specs=[vmem] * 2,
        out_specs=(vmem, vmem),
    )(*results)


def solution(mesh):
    placed = (
        P(("sky", "tm"), None),
        P(None, ("sky", "tm"), None),
        P(None, ("sky", "tm"), None),
        P(("sky", "tm")),
        P(("sky", "tm")),
        P(("sky", "tm")),
        P(None, "sky"),
        P(None, None, "sky"),
        P(None, "tm", "sky"),
        P(None, None, "tm", "sky"),
        P(None, "tm", "sky"),
        P(),
    )
    return jax.shard_map(
        per_device,
        mesh=mesh,
        in_specs=placed,
        out_specs=(P(None, "sky"), P(None, "tm", "sky")),
        check_vma=False,
    )
```

```python
import functools

import jax
import jax.numpy as jnp
from jax import lax
from jax.experimental import pallas as pl
from jax.experimental.pallas import tpu as pltpu
from jax.sharding import PartitionSpec as P

BLOCK_KNOTS = 16
SWEEPS = 3
ITERS = 2
NPAR = 5
NAX = 3
LANES = 128
REACH = 2
HOT_CAP = 4 << 20
MESH = pl.DeviceIdType.MESH
F32 = jnp.float32
BF16 = jnp.bfloat16

NN = (((1,), (0,)), ((), ()))
NT = (((1,), (1,)), ((), ()))


def iota(shape, dim):
    return lax.broadcasted_iota(jnp.int32, shape, dim)


def onehot(mask):
    return jnp.where(mask, 1.0, 0.0).astype(BF16)


def parts(x):
    high = x.astype(BF16)
    return high, (x - high.astype(F32)).astype(BF16)


def mm(a, b, dims=NN):
    return lax.dot_general(a, b, dims, preferred_element_type=F32)


def left_dot(x, hot, dims=NN):
    n = x.shape[0]
    out = mm(jnp.concatenate(parts(x), axis=0), hot, dims)
    return out[:n] + out[n:]


def spline_at(row, knot, rows):
    moment = 1.5 + (BLOCK_KNOTS - 3) * (row.astype(F32) + 0.5) / rows
    dist = jnp.abs(moment - knot.astype(F32))
    inner = 2.0 / 3.0 - dist * dist + 0.5 * dist * dist * dist
    rest = 2.0 - dist
    outer = rest * rest * rest / 6.0
    return jnp.where(dist < 1.0, inner, jnp.where(dist < 2.0, outer, 0.0))


def partner(me, i, n):
    if n & (n - 1):
        return lax.rem(me + i, n)
    out, bit = me, 1
    while bit < n:
        out = out + ((i // bit) % 2) * bit * (1 - 2 * ((me // bit) % 2))
        bit *= 2
    return out


def kernel(
    n_sky,
    n_tm,
    observed,
    att_partials,
    src_partials,
    src_slot,
    knot_block,
    live_count,
    sources,
    inverses,
    attitude,
    band_coef,
    extra_diag,
    band_offsets,
    sources_out,
    attitude_out,
    knots_all,
    coef_all,
    kb_all,
    slots_all,
    rhs_all,
    grads_all,
    rim_mine,
    rim_all,
    win_mine,
    win_all,
    win_low,
    win_high,
    near_mine,
    edge_all,
    hot_all,
    knots_send,
    knots_recv,
    coef_send,
    coef_recv,
    kb_send,
    kb_recv,
    near_send,
    near_recv,
    pass_send,
    pass_recv,
    slots_send,
    slots_recv,
    rhs_send,
    rhs_recv,
    grads_send,
    grads_recv,
    rim_send,
    rim_recv,
    win_send,
    win_recv,
    far_send,
    low_recv,
    high_recv,
):
    s = lax.axis_index("sky")
    t = lax.axis_index("tm")
    cross, rows = observed.shape
    knots_here = attitude.shape[2]
    blocks = knots_here // BLOCK_KNOTS
    span = blocks + 2 * REACH
    n_blocks = n_sky * blocks
    n_src = sources.shape[1]
    n_band = band_coef.shape[0]
    tile = win_all.shape[2]
    k16 = BLOCK_KNOTS
    per = LANES // blocks
    n_lines = (1 + n_band) * NAX
    n_near = 2 * REACH + 1

    first_t, last_t = t == 0, t == n_tm - 1
    at_low, at_high = s == 0, s == n_sky - 1
    not_first, not_last = t > 0, t < n_tm - 1
    t_up, t_down = jnp.minimum(t + 1, n_tm - 1), jnp.maximum(t - 1, 0)

    barrier = pltpu.get_barrier_semaphore()
    for i in range(n_sky - 1, 0, -1):
        pl.semaphore_signal(barrier, inc=1, device_id=(partner(s, i, n_sky), t), device_id_type=MESH)
    for i in range(n_tm - 1, 0, -1):
        pl.semaphore_signal(barrier, inc=1, device_id=(s, partner(t, i, n_tm)), device_id_type=MESH)

    def remote(src, dst, send, recv, to):
        return pltpu.make_async_remote_copy(
            src_ref=src, dst_ref=dst, send_sem=send, recv_sem=recv, device_id=to, device_id_type=MESH
        )

    def to_sky(i):
        return (partner(s, i, n_sky), t)

    def to_tm(i):
        return (s, partner(t, i, n_tm))

    def knots_copy(i):
        return remote(knots_all.at[s], knots_all.at[s], knots_send.at[i], knots_recv.at[i], to_sky(i))

    def coef_copy(i):
        return remote(coef_all.at[s], coef_all.at[s], coef_send.at[i], coef_recv.at[i], to_sky(i))

    def kb_copy(i):
        return remote(kb_all.at[s], kb_all.at[s], kb_send.at[i], kb_recv.at[i], to_sky(i))

    def near_copy(side):
        to = (s, t_up if side == 0 else t_down)
        return remote(near_mine.at[side], edge_all.at[side], near_send.at[side], near_recv.at[side], to)

    def pass_copy(side, i):
        return remote(edge_all.at[side], edge_all.at[side], pass_send.at[side, i], pass_recv.at[side], to_sky(i))

    def slots_copy(i):
        return remote(slots_all.at[t], slots_all.at[t], slots_send.at[i], slots_recv.at[i], to_tm(i))

    def rhs_copy(it, i):
        return remote(rhs_all.at[it, t], rhs_all.at[it, t], rhs_send.at[it, i], rhs_recv.at[it, i], to_tm(i))

    def grads_copy(i):
        return remote(grads_all.at[s], grads_all.at[s], grads_send.at[i], grads_recv.at[i], to_sky(i))

    def rim_copy(side, to_s, slot):
        to = (to_s, t_down if side == 0 else t_up)
        return remote(rim_mine.at[side], rim_all.at[side, slot], rim_send.at[side, to_s], rim_recv.at[side, slot], to)

    def win_copy(i):
        to = to_sky(i)
        return remote(win_mine.at[1 + to[0]], win_all.at[s], win_send.at[i], win_recv.at[i], to)

    def low_copy(slot):
        return remote(win_mine.at[n_sky + 1], win_low.at[slot], far_send.at[0], low_recv.at[slot], (0, t_up))

    def high_copy(slot):
        return remote(win_mine.at[0], win_high.at[slot], far_send.at[1], high_recv.at[slot], (n_sky - 1, t_down))

    own_knot = iota((k16, knots_here), 0) == iota((k16, knots_here), 1) % k16
    shape = (knots_here, LANES)
    fold = jnp.concatenate(
        [onehot(iota(shape, 1) == iota(shape, 0) // k16 + blocks * c) for c in range(per)], axis=0
    )

    def spread(lines):
        lines = lines + [jnp.zeros((1, knots_here), F32)] * (per - len(lines))
        return jnp.concatenate([jnp.where(own_knot, line, 0.0) for line in lines], axis=1)

    knots_all[s] = left_dot(spread([attitude[a] for a in range(NAX)]), fold)
    slot_row = src_slot[...].astype(F32)
    block_row = knot_block[...].astype(F32)
    slots_all[t] = slot_row
    kb_all[s] = block_row
    bands = [[band_coef[b, a] for a in range(NAX)] for b in range(n_band)]
    inv_diag = []
    for a in range(NAX):
        band_sum = bands[0][a]
        for b in range(1, n_band):
            band_sum = band_sum + bands[b][a]
        inv_diag.append(1.0 / (extra_diag[a] + 2.0 * band_sum))
    lines = inv_diag + [bands[b][a] * inv_diag[a] for b in range(n_band) for a in range(NAX)]
    coef = left_dot(
        jnp.concatenate([spread(lines[c : c + per]) for c in range(0, n_lines, per)], axis=0), fold
    )
    coef_all[s] = coef
    edge_lane = iota((k16, LANES), 1) // REACH
    for side in range(2):
        edge = jnp.zeros((k16, LANES), F32)
        for l in range(n_lines):
            j, c = l // per, l % per
            begin = c * blocks + (blocks - REACH if side == 0 else 0)
            moved = pltpu.roll(coef[j * k16 : (j + 1) * k16], (REACH * l - begin) % LANES, 1)
            edge = jnp.where(edge_lane == l, moved, edge)
        near_mine[side] = edge

    pl.semaphore_wait(barrier, (n_sky - 1) + (n_tm - 1))
    for i in range(n_sky - 1, 0, -1):
        knots_copy(i).start()
    for i in range(n_tm - 1, 0, -1):
        slots_copy(i).start()
    take_low, take_high = jnp.logical_and(at_high, not_first), jnp.logical_and(at_low, not_last)

    @pl.when(jnp.logical_and(at_high, not_last))
    def _():
        near_copy(0).start()

    @pl.when(jnp.logical_and(at_low, not_first))
    def _():
        near_copy(1).start()

    for i in range(n_sky - 1, 0, -1):
        kb_copy(i).start()
    for i in range(n_sky - 1, 0, -1):
        coef_copy(i).start()

    lane = iota((1, cross), 1)
    live = lane < live_count[0]

    shape = (n_src, cross)
    src_hot = onehot(iota(shape, 0).astype(F32) == slot_row)
    gap_rows = jnp.zeros((8 - NPAR, n_src), F32)
    src_list = [x for q in range(NPAR) for x in (inverses[q], gap_rows)]
    gathered = left_dot(jnp.concatenate(src_list + [sources[...], gap_rows], axis=0), src_hot)

    eye = onehot(iota((rows, rows), 0) == iota((rows, rows), 1))
    par = [mm(eye, src_partials[p], NT) for p in range(NPAR)]
    att = [mm(eye, att_partials[a], NT) for a in range(NAX)]

    def source_term(values):
        total = par[0] * values[0:1]
        for p in range(1, NPAR):
            total = total + par[p] * values[p : p + 1]
        return total

    base = jnp.transpose(observed[...]) - source_term(gathered[NPAR * 8 :])

    shape = (k16, 2 * rows)
    high, low = parts(spline_at(iota(shape, 1) % rows, iota(shape, 0), rows))
    low = jnp.where(iota(shape, 1) < rows, low.astype(F32), 0.0).astype(BF16)
    back = jnp.concatenate([high, low], axis=0)
    shape = (rows, 3 * k16)
    high, low = parts(spline_at(iota(shape, 0), iota(shape, 1) % k16, rows))
    look = jnp.where(iota(shape, 1) < 2 * k16, high.astype(F32), low.astype(F32)).astype(BF16)

    def back_dot(value):
        spread = jnp.concatenate([x * value for x in att], axis=1)
        out = mm(back, jnp.concatenate(parts(spread), axis=0))
        return out[:k16] + out[k16:]

    def look_dot(knots):
        high, low = parts(knots)
        return mm(look, jnp.concatenate([high, low, high], axis=0))

    cross_terms = [back_dot(par[q]) for q in range(NPAR)]

    def against_params(value):
        return jnp.concatenate(
            [jnp.sum(par[p] * value, axis=0, keepdims=True) for p in range(NPAR)]
            + [jnp.zeros((8 - NPAR, cross), F32)],
            axis=0,
        )

    on_base = against_params(base)

    near_row = jnp.concatenate([block_row + (m - REACH) for m in range(n_near)], axis=1)
    shape = (n_sky * LANES, n_near * cross)
    found = iota((n_sky * LANES, 1), 0)
    found = found // LANES * blocks + found % blocks
    near_hot = onehot(found.astype(F32) == near_row)
    found = iota((LANES, 1), 0) % REACH
    low_hot = onehot((found - REACH).astype(F32) == near_row)
    high_hot = onehot((found + n_blocks).astype(F32) == near_row)
    near_hot = jnp.concatenate([near_hot, low_hot, high_hot], axis=0)
    mid = slice(REACH * cross, (REACH + 1) * cross)

    def window_col(count, first):
        m = iota((count * tile, LANES), 0)
        h, at = m // tile + first, m % tile
        i = at
        for a in range(1, NAX):
            i = i - jnp.where(at >= a * span, span, 0)
        return jnp.where(at >= NAX * span, -1, h * blocks - REACH + i).astype(F32)

    line_lane = iota((k16, n_sky * LANES), 1) % LANES // blocks

    def lanes_of(tiles):
        return jnp.concatenate([tiles[:, a * cross : (a + 1) * cross] for a in range(NAX)], axis=0)

    def rows_of(lines):
        return jnp.concatenate([lines[a * k16 : (a + 1) * k16] for a in range(NAX)], axis=1)

    def pick_axes(lines, count):
        lane = iota((k16, count * tile), 1) % tile
        picked = lines[(NAX - 1) * k16 :]
        for a in range(NAX - 2, -1, -1):
            picked = jnp.where(lane < (a + 1) * span, lines[a * k16 : (a + 1) * k16], picked)
        return picked

    for i in range(1, n_tm):
        slots_copy(i).wait_recv()
    slots_row = jnp.concatenate([slots_all[i] for i in range(n_tm)], axis=1)
    slot_col = jnp.transpose(jnp.broadcast_to(slot_row, (LANES, cross)))[:, :1]
    same_source = onehot(slot_col == slots_row)

    @pl.when(take_low)
    def _():
        near_copy(0).wait_recv()
        for i in range(n_sky - 1, 0, -1):
            pass_copy(0, i).start()

    @pl.when(take_high)
    def _():
        near_copy(1).wait_recv()
        for i in range(n_sky - 1, 0, -1):
            pass_copy(1, i).start()

    def shift_rows(outs, ins):
        shape = (outs * n_band * k16, ins * k16)
        c, d = iota(shape, 0), iota(shape, 1)
        m, b = c // (n_band * k16), c // k16 % n_band
        gap = jnp.abs(d - (m + (ins - outs) // 2) * k16 - c % k16)
        offset = jnp.zeros(shape, jnp.int32)
        for i in range(n_band):
            offset = jnp.where(b == i, band_offsets[i], offset)
        hot = onehot(gap == offset)
        return jnp.concatenate([hot, hot], axis=1)

    shifts = [shift_rows(n_near - 2 * i, n_near - 2 * i + 2) for i in range(1, SWEEPS)]

    def smooth_near(first, terms):
        delta = first
        for i in range(1, SWEEPS):
            sums = mm(shifts[i - 1], jnp.concatenate(parts(jnp.concatenate(delta, axis=0)), axis=0))
            delta = []
            for m in range(n_near - 2 * i):
                at = m + i
                total = first[at]
                for b in range(n_band):
                    row = (m * n_band + b) * k16
                    total = total + terms[b][at - 1] * sums[row : row + k16]
                delta.append(total)
        return delta[0]

    def smooth(grad, inv, terms):
        first = grad * inv
        delta = first
        for sweep in range(SWEEPS - 1):
            near = jnp.concatenate([pltpu.roll(delta, 1, 1), delta, pltpu.roll(delta, tile - 1, 1)], axis=0)
            sums = mm(shifts[-1], jnp.concatenate(parts(near), axis=0))
            delta = first
            for b in range(n_band):
                delta = delta + terms[b] * sums[b * k16 : (b + 1) * k16]
        return delta

    for i in range(1, n_sky):
        knots_copy(i).wait_recv()
    knots = jnp.concatenate([knots_all[h] for h in range(n_sky)], axis=1)
    knots = jnp.concatenate([jnp.where(line_lane == a, knots, 0.0) for a in range(NAX)], axis=0)
    fetched = rows_of(left_dot(knots, near_hot[: n_sky * LANES, mid]))

    def send_rhs(it, fetched, on_base):
        out = []
        for q in range(NPAR):
            term = jnp.sum(fetched * cross_terms[q], axis=0, keepdims=True)
            total = term[:, :cross]
            for a in range(1, NAX):
                total = total + term[:, a * cross : (a + 1) * cross]
            out.append(total)
        out.append(jnp.zeros((8 - NPAR, cross), F32))
        rhs_all[it, t] = jnp.where(live, on_base - jnp.concatenate(out, axis=0), 0.0)
        for i in range(n_tm - 1, 0, -1):
            rhs_copy(it, i).start()

    def grads_of(base, fetched):
        seen = look_dot(fetched)
        resid = base
        for a in range(NAX):
            resid = resid - att[a] * seen[:, a * cross : (a + 1) * cross]
        return back_dot(jnp.where(live, resid, 0.0))

    def wait_rhs(it):
        for i in range(1, n_tm):
            rhs_copy(it, i).wait_recv()
        return jnp.concatenate([rhs_all[it, i] for i in range(n_tm)], axis=1)

    live_all = jnp.concatenate([live] * NAX, axis=1)

    def step_of(rhs):
        normal = left_dot(rhs, same_source, NT)
        return [
            jnp.sum(gathered[q * 8 : (q + 1) * 8] * normal, axis=0, keepdims=True)
            for q in range(NPAR)
        ]

    def move_grads(grads, step):
        total = jnp.concatenate([step[0]] * NAX, axis=1) * cross_terms[0]
        for q in range(1, NPAR):
            total = total + jnp.concatenate([step[q]] * NAX, axis=1) * cross_terms[q]
        return grads - jnp.where(live_all, total, 0.0)

    send_rhs(0, fetched, on_base)
    grads = grads_of(base, fetched)

    for i in range(1, n_sky):
        kb_copy(i).wait_recv()

    prebuilt = hot_all.shape[0] == n_sky

    block_col = jnp.transpose(jnp.broadcast_to(block_row, (LANES, cross)))
    near_col = jnp.concatenate([block_col + (m - REACH) for m in range(n_near)], axis=0)

    def sender_hot(h):
        return onehot(near_col == kb_all[h])

    if prebuilt:
        for h in range(n_sky):
            hot_all[h] = sender_hot(h)

    rim_row = iota((k16, cross), 0)
    rim_block = jnp.where(rim_row < 8, rim_row, n_blocks - REACH - 8 + rim_row)
    rim_hot = onehot(
        jnp.logical_and(rim_row % 8 < REACH, rim_block.astype(F32) == block_row)
    )

    rhs = wait_rhs(0)
    rhs_total = rhs
    step = step_of(rhs)
    grads = move_grads(grads, step)
    grads_all[s] = grads
    for i in range(n_sky - 1, 0, -1):
        grads_copy(i).start()

    high, low = parts(lanes_of(grads))
    gap_rows = jnp.zeros((LANES - NAX * k16, cross), BF16)
    rims = mm(rim_hot, jnp.concatenate([high, gap_rows], axis=0), NT) + mm(
        rim_hot, jnp.concatenate([low, gap_rows], axis=0), NT
    )
    rim_mine[0] = rims[:REACH]
    rim_mine[1] = rims[8 : 8 + REACH]

    @pl.when(not_first)
    def _():
        for i in range(n_sky - 1, -1, -1):
            rim_copy(0, partner(s, i, n_sky), s).start()

    @pl.when(not_last)
    def _():
        for i in range(n_sky - 1, -1, -1):
            rim_copy(1, partner(s, i, n_sky), s).start()

    base = base - source_term(jnp.concatenate(step, axis=0))
    on_base = against_params(base)
    for i in range(1, n_sky):
        coef_copy(i).wait_recv()

    @pl.when(jnp.logical_and(not_first, jnp.logical_not(at_high)))
    def _():
        pass_copy(0, 1).wait_recv()

    @pl.when(jnp.logical_and(not_last, jnp.logical_not(at_low)))
    def _():
        pass_copy(1, 1).wait_recv()

    @pl.when(first_t)
    def _():
        edge_all[0] = jnp.zeros(edge_all.shape[1:], F32)
        rim_all[1] = jnp.zeros(rim_all.shape[1:], F32)

    @pl.when(last_t)
    def _():
        edge_all[1] = jnp.zeros(edge_all.shape[1:], F32)
        rim_all[0] = jnp.zeros(rim_all.shape[1:], F32)

    def coef_lines(first, last):
        out = []
        for l in range(first, last):
            j, c = l // per, l % per
            line = jnp.concatenate([coef_all[h, j * k16 : (j + 1) * k16] for h in range(n_sky)], axis=1)
            ends = [jnp.where(edge_lane == l, edge_all[side], 0.0) for side in range(2)]
            out.append(jnp.concatenate([jnp.where(line_lane == c, line, 0.0)] + ends, axis=1))
        return jnp.concatenate(out, axis=0)

    inv_lines, term_lines = coef_lines(0, NAX), coef_lines(NAX, n_lines)
    inv_near = left_dot(inv_lines, near_hot)
    got = left_dot(term_lines, near_hot[:, cross : (n_near - 1) * cross])
    terms_near = [
        [
            rows_of(got[b * NAX * k16 : (b + 1) * NAX * k16, m * cross : (m + 1) * cross])
            for m in range(n_near - 2)
        ]
        for b in range(n_band)
    ]

    shape = (2 * REACH * LANES, 2 * tile)
    c, d = iota(shape, 0), iota(shape, 1)
    r, c = c // LANES, c % LANES
    spot = (c // k16) * span + jnp.where(r < REACH, r, tile + blocks + r)
    rim_fold = onehot(jnp.logical_and(c < NAX * k16, d == spot))
    rim_knot = iota((k16, LANES), 0) == iota((k16, LANES), 1) % k16

    @pl.when(not_last)
    def _():
        for i in range(n_sky):
            rim_copy(0, i, i).wait_recv()

    @pl.when(not_first)
    def _():
        for i in range(n_sky):
            rim_copy(1, i, i).wait_recv()

    rim_rows = []
    for side in (1, 0):
        total = rim_all[side, 0]
        for i in range(1, n_sky):
            total = total + rim_all[side, i]
        rim_rows = rim_rows + [total[i : i + 1] for i in range(REACH)]
    rim_cols = jnp.transpose(
        jnp.concatenate(rim_rows + [jnp.zeros((LANES - 2 * REACH, LANES), F32)], axis=0)
    )
    found = iota((LANES, 1), 0)
    found = jnp.where(found < REACH, found - REACH, found + n_blocks - REACH)
    found = jnp.where(iota((LANES, 1), 0) < 2 * REACH, found, -8 * REACH)
    grad = left_dot(rim_cols[: NAX * k16], onehot(found.astype(F32) == near_row))

    group = 2 if n_sky % 2 == 0 else 1

    def scatter(j, total):
        home = partner(s // group, j, n_sky // group) * group
        lines = jnp.concatenate([lanes_of(grads_all[home + x]) for x in range(group)], axis=1)
        hots = [hot_all[home + x] if prebuilt else sender_hot(home + x) for x in range(group)]
        return total + left_dot(lines, jnp.concatenate(hots, axis=1), NT)

    for x in range(1, group):
        grads_copy(x).wait_recv()
    grad = scatter(0, grad)

    def add_group(j, total):
        for x in range(group):
            grads_copy(j * group + x).wait_recv()
        return scatter(j, total)

    if prebuilt:
        for j in range(1, n_sky // group):
            grad = add_group(j, grad)
    else:
        grad = lax.fori_loop(1, n_sky // group, add_group, grad)

    first = grad * inv_near
    moved = smooth_near(
        [rows_of(first[:, m * cross : (m + 1) * cross]) for m in range(n_near)], terms_near
    )
    fetched = fetched + moved
    send_rhs(1, fetched, on_base)
    grads = grads_of(base, fetched)
    win_hot = onehot(window_col(n_sky + 2, -1) == block_row)
    own_col = window_col(1, s)
    own_row = jnp.concatenate([kb_all[h] for h in range(n_sky)], axis=1)
    own_hot = onehot(jnp.concatenate([own_col] * n_sky, axis=1) == own_row)
    lines = jnp.concatenate([lanes_of(grads_all[h]) for h in range(n_sky)], axis=1)
    grad_own = pick_axes(left_dot(lines, own_hot, NT), 1)
    rim_tiles = left_dot(
        jnp.concatenate([jnp.where(rim_knot, row, 0.0) for row in rim_rows], axis=1), rim_fold
    )
    grad_own = grad_own + jnp.where(at_low, rim_tiles[:, :tile], 0.0)
    grad_own = grad_own + jnp.where(at_high, rim_tiles[:, tile:], 0.0)
    rhs = wait_rhs(1)
    rhs_total = rhs_total + rhs
    grads = move_grads(grads, step_of(rhs))
    picked = pick_axes(left_dot(lanes_of(grads), win_hot, NT), n_sky + 2)
    for h in range(n_sky + 2):
        win_mine[h] = picked[:, h * tile : (h + 1) * tile]

    for i in range(n_sky - 1, 0, -1):
        win_copy(i).start()

    @pl.when(not_last)
    def _():
        low_copy(s).start()

    @pl.when(not_first)
    def _():
        high_copy(s).start()

    win_all[s] = win_mine[1 + s]
    from_low, from_high = jnp.logical_and(at_low, not_first), jnp.logical_and(at_high, not_last)

    @pl.when(jnp.logical_not(from_low))
    def _():
        win_low[...] = jnp.zeros(win_low.shape, F32)

    @pl.when(jnp.logical_not(from_high))
    def _():
        win_high[...] = jnp.zeros(win_high.shape, F32)

    full_hot = onehot(iota((n_src, n_tm * cross), 0).astype(F32) == slots_row)
    normal_all = left_dot(rhs_total, full_hot, NT)[:NPAR]
    steps = [jnp.sum(inverses[q] * normal_all, axis=0, keepdims=True) for q in range(NPAR)]
    sources_out[...] = sources[...] + jnp.concatenate(steps, axis=0)
    shape = (n_sky * LANES, tile)
    m, at = iota((n_sky * LANES, 1), 0), iota((1, tile), 1)
    i = at
    for a in range(1, NAX):
        i = i - jnp.where(at >= a * span, span, 0)
    own_place = jnp.where(at >= NAX * span, -8 * REACH, s * blocks - REACH + i).astype(F32)
    found = [
        m // LANES * blocks + m % blocks,
        iota((LANES, 1), 0) % REACH - REACH,
        iota((LANES, 1), 0) % REACH + n_blocks,
    ]
    coef_hot = jnp.concatenate([onehot(x.astype(F32) == own_place) for x in found], axis=0)
    got = left_dot(jnp.concatenate([inv_lines, term_lines], axis=0), coef_hot)
    own = [pick_axes(got[b * NAX * k16 : (b + 1) * NAX * k16], 1) for b in range(n_band + 1)]
    inv_own, terms_own = own[0], own[1:]
    shape = (knots_here, tile)
    unfold = jnp.concatenate(
        [onehot(iota(shape, 1) == (iota(shape, 0) // k16) + (span * a + REACH)) for a in range(NAX)], axis=0
    )

    for i in range(1, n_sky):
        win_copy(i).wait_recv()

    @pl.when(from_low)
    def _():
        for i in range(n_sky):
            low_copy(i).wait_recv()

    @pl.when(from_high)
    def _():
        for i in range(n_sky):
            high_copy(i).wait_recv()

    grad = grad_own
    for i in range(n_sky):
        grad = grad + (win_all[i] + win_low[i] + win_high[i])
    moved = smooth(grad, inv_own, terms_own)

    line = left_dot(moved, unfold, NT)
    for a in range(NAX):
        own = jnp.where(own_knot, line[:, a * knots_here : (a + 1) * knots_here], 0.0)
        attitude_out[a] = attitude[a] + jnp.sum(own, axis=0, keepdims=True)

    for i in range(1, n_sky):
        knots_copy(i).wait_send()
        coef_copy(i).wait_send()
        kb_copy(i).wait_send()
        grads_copy(i).wait_send()
        win_copy(i).wait_send()
    for i in range(1, n_tm):
        slots_copy(i).wait_send()
        for it in range(ITERS):
            rhs_copy(it, i).wait_send()

    @pl.when(jnp.logical_and(at_high, not_last))
    def _():
        near_copy(0).wait_send()

    @pl.when(jnp.logical_and(at_low, not_first))
    def _():
        near_copy(1).wait_send()

    @pl.when(take_low)
    def _():
        for i in range(1, n_sky):
            pass_copy(0, i).wait_send()

    @pl.when(take_high)
    def _():
        for i in range(1, n_sky):
            pass_copy(1, i).wait_send()

    @pl.when(not_first)
    def _():
        for i in range(n_sky):
            rim_copy(0, i, s).wait_send()
        high_copy(s).wait_send()

    @pl.when(not_last)
    def _():
        for i in range(n_sky):
            rim_copy(1, i, s).wait_send()
        low_copy(s).wait_send()


def finish(sources_in, attitude_in, sources_out, attitude_out):
    sources_out[...] = sources_in[...]
    attitude_out[...] = attitude_in[...]


def per_device(
    observed,
    att_partials,
    src_partials,
    src_slot,
    knot_block,
    live_count,
    sources,
    inverses,
    attitude,
    band_coef,
    extra_diag,
    band_offsets,
):
    n_sky, n_tm = lax.axis_size("sky"), lax.axis_size("tm")
    blocks = attitude.shape[2] // BLOCK_KNOTS
    cross = src_slot.shape[0]
    k16 = BLOCK_KNOTS
    tile = -(-NAX * (blocks + 2 * REACH) // LANES) * LANES
    n_tiles = -(-(1 + band_coef.shape[0]) * NAX * blocks // LANES)
    n_near = (2 * REACH + 1) * cross
    n_hot = n_sky if n_sky * n_near * cross * 2 <= HOT_CAP else 1
    vmem = pl.BlockSpec(memory_space=pltpu.VMEM)
    smem = pl.BlockSpec(memory_space=pltpu.SMEM)
    dma = pltpu.SemaphoreType.DMA
    results = pl.pallas_call(
        functools.partial(kernel, n_sky, n_tm),
        out_shape=(
            jax.ShapeDtypeStruct(sources.shape, F32),
            jax.ShapeDtypeStruct(attitude.shape, F32),
        ),
        in_specs=[vmem] * 5 + [smem] + [vmem] * 5 + [smem],
        out_specs=(vmem, vmem),
        scratch_shapes=[
            pltpu.VMEM((n_sky, k16, LANES), F32),
            pltpu.VMEM((n_sky, n_tiles * k16, LANES), F32),
            pltpu.VMEM((n_sky, 1, cross), F32),
            pltpu.VMEM((n_tm, 1, cross), F32),
            pltpu.VMEM((ITERS, n_tm, 8, cross), F32),
            pltpu.VMEM((n_sky, k16, NAX * cross), F32),
            pltpu.VMEM((2, REACH, LANES), F32),
            pltpu.VMEM((2, n_sky, REACH, LANES), F32),
            pltpu.VMEM((n_sky + 2, k16, tile), F32),
            pltpu.VMEM((n_sky, k16, tile), F32),
            pltpu.VMEM((n_sky, k16, tile), F32),
            pltpu.VMEM((n_sky, k16, tile), F32),
            pltpu.VMEM((2, k16, LANES), F32),
            pltpu.VMEM((2, k16, LANES), F32),
            pltpu.VMEM((n_hot, n_near, cross), BF16),
            dma((n_sky,)),
            dma((n_sky,)),
            dma((n_sky,)),
            dma((n_sky,)),
            dma((n_sky,)),
            dma((n_sky,)),
            dma((2,)),
            dma((2,)),
            dma((2, n_sky)),
            dma((2,)),
            dma((n_tm,)),
            dma((n_tm,)),
            dma((ITERS, n_tm)),
            dma((ITERS, n_tm)),
            dma((n_sky,)),
            dma((n_sky,)),
            dma((2, n_sky)),
            dma((2, n_sky)),
            dma((n_sky,)),
            dma((n_sky,)),
            dma((2,)),
            dma((n_sky,)),
            dma((n_sky,)),
        ],
        compiler_params=pltpu.CompilerParams(
            collective_id=0, has_side_effects=True
        ),
    )(
        observed,
        att_partials,
        src_partials,
        src_slot[None, :],
        knot_block[None, :],
        live_count,
        sources,
        inverses,
        attitude,
        band_coef,
        extra_diag,
        band_offsets,
    )
    return pl.pallas_call(
        finish,
        out_shape=(
            jax.ShapeDtypeStruct(sources.shape, F32),
            jax.ShapeDtypeStruct(attitude.shape, F32),
        ),
        in_specs=[vmem] * 2,
        out_specs=(vmem, vmem),
    )(*results)


def solution(mesh):
    placed = (
        P(("sky", "tm"), None),
        P(None, ("sky", "tm"), None),
        P(None, ("sky", "tm"), None),
        P(("sky", "tm")),
        P(("sky", "tm")),
        P(("sky", "tm")),
        P(None, "sky"),
        P(None, None, "sky"),
        P(None, "tm", "sky"),
        P(None, None, "tm", "sky"),
        P(None, "tm", "sky"),
        P(),
    )
    return jax.shard_map(
        per_device,
        mesh=mesh,
        in_specs=placed,
        out_specs=(P(None, "sky"), P(None, "tm", "sky")),
        check_vma=False,
    )
```

```python
import functools

import jax
import jax.numpy as jnp
from jax import lax
from jax.experimental import pallas as pl
from jax.experimental.pallas import tpu as pltpu
from jax.sharding import PartitionSpec as P

BLOCK_KNOTS = 16
SWEEPS = 3
ITERS = 2
NPAR = 5
NAX = 3
LANES = 128
REACH = 2
HOT_CAP = 4 << 20
VMEM_LIMIT = 61960 << 10
MESH = pl.DeviceIdType.MESH
F32 = jnp.float32
BF16 = jnp.bfloat16

NN = (((1,), (0,)), ((), ()))
NT = (((1,), (1,)), ((), ()))


def iota(shape, dim):
    return lax.broadcasted_iota(jnp.int32, shape, dim)


def onehot(mask):
    return jnp.where(mask, 1.0, 0.0).astype(BF16)


def parts(x):
    high = x.astype(BF16)
    return high, (x - high.astype(F32)).astype(BF16)


def mm(a, b, dims=NN):
    return lax.dot_general(a, b, dims, preferred_element_type=F32)


def left_dot(x, hot, dims=NN):
    n = x.shape[0]
    out = mm(jnp.concatenate(parts(x), axis=0), hot, dims)
    return out[:n] + out[n:]


def spline_at(row, knot, rows):
    moment = 1.5 + (BLOCK_KNOTS - 3) * (row.astype(F32) + 0.5) / rows
    dist = jnp.abs(moment - knot.astype(F32))
    inner = 2.0 / 3.0 - dist * dist + 0.5 * dist * dist * dist
    rest = 2.0 - dist
    outer = rest * rest * rest / 6.0
    return jnp.where(dist < 1.0, inner, jnp.where(dist < 2.0, outer, 0.0))


def partner(me, i, n):
    if n & (n - 1):
        return lax.rem(me + i, n)
    out, bit = me, 1
    while bit < n:
        out = out + ((i // bit) % 2) * bit * (1 - 2 * ((me // bit) % 2))
        bit *= 2
    return out


def kernel(
    n_sky,
    n_tm,
    observed_in,
    att_partials_in,
    src_partials_in,
    src_slot_in,
    knot_block_in,
    live_count_in,
    sources_in,
    inverses_in,
    attitude_in,
    band_coef_in,
    extra_diag_in,
    band_offsets_in,
    sources_out,
    attitude_out,
    observed,
    att_partials,
    src_partials,
    src_slot,
    knot_block,
    live_count,
    sources,
    inverses,
    attitude,
    band_coef,
    extra_diag,
    band_offsets,
    input_sem,
    knots_all,
    coef_all,
    kb_all,
    slots_all,
    rhs_all,
    grads_all,
    rim_mine,
    rim_all,
    win_mine,
    win_all,
    win_low,
    win_high,
    near_mine,
    edge_all,
    hot_all,
    knots_send,
    knots_recv,
    coef_send,
    coef_recv,
    kb_send,
    kb_recv,
    near_send,
    near_recv,
    pass_send,
    pass_recv,
    slots_send,
    slots_recv,
    rhs_send,
    rhs_recv,
    grads_send,
    grads_recv,
    rim_send,
    rim_recv,
    win_send,
    win_recv,
    far_send,
    low_recv,
    high_recv,
):
    s = lax.axis_index("sky")
    t = lax.axis_index("tm")
    cross, rows = observed.shape
    knots_here = attitude.shape[2]
    blocks = knots_here // BLOCK_KNOTS
    span = blocks + 2 * REACH
    n_blocks = n_sky * blocks
    n_src = sources.shape[1]
    n_band = band_coef.shape[0]
    tile = win_all.shape[2]
    k16 = BLOCK_KNOTS
    per = LANES // blocks
    n_lines = (1 + n_band) * NAX
    n_near = 2 * REACH + 1

    first_t, last_t = t == 0, t == n_tm - 1
    at_low, at_high = s == 0, s == n_sky - 1
    not_first, not_last = t > 0, t < n_tm - 1
    t_up, t_down = jnp.minimum(t + 1, n_tm - 1), jnp.maximum(t - 1, 0)

    barrier = pltpu.get_barrier_semaphore()
    for i in range(n_sky - 1, 0, -1):
        pl.semaphore_signal(barrier, inc=1, device_id=(partner(s, i, n_sky), t), device_id_type=MESH)
    for i in range(n_tm - 1, 0, -1):
        pl.semaphore_signal(barrier, inc=1, device_id=(s, partner(t, i, n_tm)), device_id_type=MESH)

    pairs = (
        (attitude_in, attitude),
        (band_coef_in, band_coef),
        (extra_diag_in, extra_diag),
        (src_slot_in, src_slot),
        (knot_block_in, knot_block),
        (src_partials_in, src_partials),
        (att_partials_in, att_partials),
        (inverses_in, inverses),
        (sources_in, sources),
        (observed_in, observed),
        (live_count_in, live_count),
        (band_offsets_in, band_offsets),
    )
    loads = [
        pltpu.make_async_copy(source, place, input_sem.at[i])
        for i, (source, place) in enumerate(pairs)
    ]
    for load in loads:
        load.start()

    def remote(src, dst, send, recv, to):
        return pltpu.make_async_remote_copy(
            src_ref=src, dst_ref=dst, send_sem=send, recv_sem=recv, device_id=to, device_id_type=MESH
        )

    def to_sky(i):
        return (partner(s, i, n_sky), t)

    def to_tm(i):
        return (s, partner(t, i, n_tm))

    def knots_copy(i):
        return remote(knots_all.at[s], knots_all.at[s], knots_send.at[i], knots_recv.at[i], to_sky(i))

    def coef_copy(i):
        return remote(coef_all.at[s], coef_all.at[s], coef_send.at[i], coef_recv.at[i], to_sky(i))

    def kb_copy(i):
        return remote(kb_all.at[s], kb_all.at[s], kb_send.at[i], kb_recv.at[i], to_sky(i))

    def near_copy(side):
        to = (s, t_up if side == 0 else t_down)
        return remote(near_mine.at[side], edge_all.at[side], near_send.at[side], near_recv.at[side], to)

    def pass_copy(side, i):
        return remote(edge_all.at[side], edge_all.at[side], pass_send.at[side, i], pass_recv.at[side], to_sky(i))

    def slots_copy(i):
        return remote(slots_all.at[t], slots_all.at[t], slots_send.at[i], slots_recv.at[i], to_tm(i))

    def rhs_copy(it, i):
        return remote(rhs_all.at[it, t], rhs_all.at[it, t], rhs_send.at[it, i], rhs_recv.at[it, i], to_tm(i))

    def grads_copy(i):
        return remote(grads_all.at[s], grads_all.at[s], grads_send.at[i], grads_recv.at[i], to_sky(i))

    def rim_copy(side, to_s, slot):
        to = (to_s, t_down if side == 0 else t_up)
        return remote(rim_mine.at[side], rim_all.at[side, slot], rim_send.at[side, to_s], rim_recv.at[side, slot], to)

    def win_copy(i):
        to = to_sky(i)
        return remote(win_mine.at[1 + to[0]], win_all.at[s], win_send.at[i], win_recv.at[i], to)

    def low_copy(slot):
        return remote(win_mine.at[n_sky + 1], win_low.at[slot], far_send.at[0], low_recv.at[slot], (0, t_up))

    def high_copy(slot):
        return remote(win_mine.at[0], win_high.at[slot], far_send.at[1], high_recv.at[slot], (n_sky - 1, t_down))

    for load in loads[:5]:
        load.wait()
    own_knot = iota((k16, knots_here), 0) == iota((k16, knots_here), 1) % k16
    shape = (knots_here, LANES)
    fold = jnp.concatenate(
        [onehot(iota(shape, 1) == iota(shape, 0) // k16 + blocks * c) for c in range(per)], axis=0
    )

    def spread(lines):
        lines = lines + [jnp.zeros((1, knots_here), F32)] * (per - len(lines))
        return jnp.concatenate([jnp.where(own_knot, line, 0.0) for line in lines], axis=1)

    knots_all[s] = left_dot(spread([attitude[a] for a in range(NAX)]), fold)
    slot_row = src_slot[...].astype(F32)
    block_row = knot_block[...].astype(F32)
    slots_all[t] = slot_row
    kb_all[s] = block_row
    bands = [[band_coef[b, a] for a in range(NAX)] for b in range(n_band)]
    inv_diag = []
    for a in range(NAX):
        band_sum = bands[0][a]
        for b in range(1, n_band):
            band_sum = band_sum + bands[b][a]
        inv_diag.append(1.0 / (extra_diag[a] + 2.0 * band_sum))
    lines = inv_diag + [bands[b][a] * inv_diag[a] for b in range(n_band) for a in range(NAX)]
    coef = left_dot(
        jnp.concatenate([spread(lines[c : c + per]) for c in range(0, n_lines, per)], axis=0), fold
    )
    coef_all[s] = coef
    edge_lane = iota((k16, LANES), 1) // REACH
    for side in range(2):
        edge = jnp.zeros((k16, LANES), F32)
        for l in range(n_lines):
            j, c = l // per, l % per
            begin = c * blocks + (blocks - REACH if side == 0 else 0)
            moved = pltpu.roll(coef[j * k16 : (j + 1) * k16], (REACH * l - begin) % LANES, 1)
            edge = jnp.where(edge_lane == l, moved, edge)
        near_mine[side] = edge

    pl.semaphore_wait(barrier, (n_sky - 1) + (n_tm - 1))
    for i in range(n_sky - 1, 0, -1):
        knots_copy(i).start()
    for i in range(n_tm - 1, 0, -1):
        slots_copy(i).start()
    take_low, take_high = jnp.logical_and(at_high, not_first), jnp.logical_and(at_low, not_last)

    @pl.when(jnp.logical_and(at_high, not_last))
    def _():
        near_copy(0).start()

    @pl.when(jnp.logical_and(at_low, not_first))
    def _():
        near_copy(1).start()

    for i in range(n_sky - 1, 0, -1):
        kb_copy(i).start()
    for i in range(n_sky - 1, 0, -1):
        coef_copy(i).start()

    for load in loads[5:]:
        load.wait()
    lane = iota((1, cross), 1)
    live = lane < live_count[0]

    shape = (n_src, cross)
    src_hot = onehot(iota(shape, 0).astype(F32) == slot_row)
    gap_rows = jnp.zeros((8 - NPAR, n_src), F32)
    src_list = [x for q in range(NPAR) for x in (inverses[q], gap_rows)]
    gathered = left_dot(jnp.concatenate(src_list + [sources[...], gap_rows], axis=0), src_hot)

    eye = onehot(iota((rows, rows), 0) == iota((rows, rows), 1))
    par = [mm(eye, src_partials[p], NT) for p in range(NPAR)]
    att = [mm(eye, att_partials[a], NT) for a in range(NAX)]

    def source_term(values):
        total = par[0] * values[0:1]
        for p in range(1, NPAR):
            total = total + par[p] * values[p : p + 1]
        return total

    base = jnp.transpose(observed[...]) - source_term(gathered[NPAR * 8 :])

    shape = (k16, 2 * rows)
    high, low = parts(spline_at(iota(shape, 1) % rows, iota(shape, 0), rows))
    low = jnp.where(iota(shape, 1) < rows, low.astype(F32), 0.0).astype(BF16)
    back = jnp.concatenate([high, low], axis=0)
    shape = (rows, 3 * k16)
    high, low = parts(spline_at(iota(shape, 0), iota(shape, 1) % k16, rows))
    look = jnp.where(iota(shape, 1) < 2 * k16, high.astype(F32), low.astype(F32)).astype(BF16)

    def back_dot(value):
        spread = jnp.concatenate([x * value for x in att], axis=1)
        out = mm(back, jnp.concatenate(parts(spread), axis=0))
        return out[:k16] + out[k16:]

    def look_dot(knots):
        high, low = parts(knots)
        return mm(look, jnp.concatenate([high, low, high], axis=0))

    cross_terms = [back_dot(par[q]) for q in range(NPAR)]

    def against_params(value):
        return jnp.concatenate(
            [jnp.sum(par[p] * value, axis=0, keepdims=True) for p in range(NPAR)]
            + [jnp.zeros((8 - NPAR, cross), F32)],
            axis=0,
        )

    on_base = against_params(base)

    near_row = jnp.concatenate([block_row + (m - REACH) for m in range(n_near)], axis=1)
    shape = (n_sky * LANES, n_near * cross)
    found = iota((n_sky * LANES, 1), 0)
    found = found // LANES * blocks + found % blocks
    near_hot = onehot(found.astype(F32) == near_row)
    found = iota((LANES, 1), 0) % REACH
    low_hot = onehot((found - REACH).astype(F32) == near_row)
    high_hot = onehot((found + n_blocks).astype(F32) == near_row)
    near_hot = jnp.concatenate([near_hot, low_hot, high_hot], axis=0)
    mid = slice(REACH * cross, (REACH + 1) * cross)

    def window_col(count, first):
        m = iota((count * tile, LANES), 0)
        h, at = m // tile + first, m % tile
        i = at
        for a in range(1, NAX):
            i = i - jnp.where(at >= a * span, span, 0)
        return jnp.where(at >= NAX * span, -1, h * blocks - REACH + i).astype(F32)

    line_lane = iota((k16, n_sky * LANES), 1) % LANES // blocks

    def lanes_of(tiles):
        return jnp.concatenate([tiles[:, a * cross : (a + 1) * cross] for a in range(NAX)], axis=0)

    def rows_of(lines):
        return jnp.concatenate([lines[a * k16 : (a + 1) * k16] for a in range(NAX)], axis=1)

    def pick_axes(lines, count):
        lane = iota((k16, count * tile), 1) % tile
        picked = lines[(NAX - 1) * k16 :]
        for a in range(NAX - 2, -1, -1):
            picked = jnp.where(lane < (a + 1) * span, lines[a * k16 : (a + 1) * k16], picked)
        return picked

    for i in range(1, n_tm):
        slots_copy(i).wait_recv()
    slots_row = jnp.concatenate([slots_all[i] for i in range(n_tm)], axis=1)
    slot_col = jnp.transpose(jnp.broadcast_to(slot_row, (LANES, cross)))[:, :1]
    same_source = onehot(slot_col == slots_row)

    @pl.when(take_low)
    def _():
        near_copy(0).wait_recv()
        for i in range(n_sky - 1, 0, -1):
            pass_copy(0, i).start()

    @pl.when(take_high)
    def _():
        near_copy(1).wait_recv()
        for i in range(n_sky - 1, 0, -1):
            pass_copy(1, i).start()

    def shift_rows(outs, ins):
        shape = (outs * n_band * k16, ins * k16)
        c, d = iota(shape, 0), iota(shape, 1)
        m, b = c // (n_band * k16), c // k16 % n_band
        gap = jnp.abs(d - (m + (ins - outs) // 2) * k16 - c % k16)
        offset = jnp.zeros(shape, jnp.int32)
        for i in range(n_band):
            offset = jnp.where(b == i, band_offsets[i], offset)
        hot = onehot(gap == offset)
        return jnp.concatenate([hot, hot], axis=1)

    shifts = [shift_rows(n_near - 2 * i, n_near - 2 * i + 2) for i in range(1, SWEEPS)]

    def smooth_near(first, terms):
        delta = first
        for i in range(1, SWEEPS):
            sums = mm(shifts[i - 1], jnp.concatenate(parts(jnp.concatenate(delta, axis=0)), axis=0))
            delta = []
            for m in range(n_near - 2 * i):
                at = m + i
                total = first[at]
                for b in range(n_band):
                    row = (m * n_band + b) * k16
                    total = total + terms[b][at - 1] * sums[row : row + k16]
                delta.append(total)
        return delta[0]

    def smooth(grad, inv, terms):
        first = grad * inv
        delta = first
        for sweep in range(SWEEPS - 1):
            near = jnp.concatenate([pltpu.roll(delta, 1, 1), delta, pltpu.roll(delta, tile - 1, 1)], axis=0)
            sums = mm(shifts[-1], jnp.concatenate(parts(near), axis=0))
            delta = first
            for b in range(n_band):
                delta = delta + terms[b] * sums[b * k16 : (b + 1) * k16]
        return delta

    for i in range(1, n_sky):
        knots_copy(i).wait_recv()
    knots = jnp.concatenate([knots_all[h] for h in range(n_sky)], axis=1)
    knots = jnp.concatenate([jnp.where(line_lane == a, knots, 0.0) for a in range(NAX)], axis=0)
    fetched = rows_of(left_dot(knots, near_hot[: n_sky * LANES, mid]))

    def send_rhs(it, fetched, on_base):
        out = []
        for q in range(NPAR):
            term = jnp.sum(fetched * cross_terms[q], axis=0, keepdims=True)
            total = term[:, :cross]
            for a in range(1, NAX):
                total = total + term[:, a * cross : (a + 1) * cross]
            out.append(total)
        out.append(jnp.zeros((8 - NPAR, cross), F32))
        rhs_all[it, t] = jnp.where(live, on_base - jnp.concatenate(out, axis=0), 0.0)
        for i in range(n_tm - 1, 0, -1):
            rhs_copy(it, i).start()

    def grads_of(base, fetched):
        seen = look_dot(fetched)
        resid = base
        for a in range(NAX):
            resid = resid - att[a] * seen[:, a * cross : (a + 1) * cross]
        return back_dot(jnp.where(live, resid, 0.0))

    def wait_rhs(it):
        for i in range(1, n_tm):
            rhs_copy(it, i).wait_recv()
        return jnp.concatenate([rhs_all[it, i] for i in range(n_tm)], axis=1)

    live_all = jnp.concatenate([live] * NAX, axis=1)

    def step_of(rhs):
        normal = left_dot(rhs, same_source, NT)
        return [
            jnp.sum(gathered[q * 8 : (q + 1) * 8] * normal, axis=0, keepdims=True)
            for q in range(NPAR)
        ]

    def move_grads(grads, step):
        total = jnp.concatenate([step[0]] * NAX, axis=1) * cross_terms[0]
        for q in range(1, NPAR):
            total = total + jnp.concatenate([step[q]] * NAX, axis=1) * cross_terms[q]
        return grads - jnp.where(live_all, total, 0.0)

    send_rhs(0, fetched, on_base)
    grads = grads_of(base, fetched)

    for i in range(1, n_sky):
        kb_copy(i).wait_recv()

    prebuilt = hot_all.shape[0] == n_sky

    block_col = jnp.transpose(jnp.broadcast_to(block_row, (LANES, cross)))
    near_col = jnp.concatenate([block_col + (m - REACH) for m in range(n_near)], axis=0)

    def sender_hot(h):
        return onehot(near_col == kb_all[h])

    if prebuilt:
        for h in range(n_sky):
            hot_all[h] = sender_hot(h)

    rim_row = iota((k16, cross), 0)
    rim_block = jnp.where(rim_row < 8, rim_row, n_blocks - REACH - 8 + rim_row)
    rim_hot = onehot(
        jnp.logical_and(rim_row % 8 < REACH, rim_block.astype(F32) == block_row)
    )

    rhs = wait_rhs(0)
    rhs_total = rhs
    step = step_of(rhs)
    grads = move_grads(grads, step)
    grads_all[s] = grads
    for i in range(n_sky - 1, 0, -1):
        grads_copy(i).start()

    high, low = parts(lanes_of(grads))
    gap_rows = jnp.zeros((LANES - NAX * k16, cross), BF16)
    rims = mm(rim_hot, jnp.concatenate([high, gap_rows], axis=0), NT) + mm(
        rim_hot, jnp.concatenate([low, gap_rows], axis=0), NT
    )
    rim_mine[0] = rims[:REACH]
    rim_mine[1] = rims[8 : 8 + REACH]

    @pl.when(not_first)
    def _():
        for i in range(n_sky - 1, -1, -1):
            rim_copy(0, partner(s, i, n_sky), s).start()

    @pl.when(not_last)
    def _():
        for i in range(n_sky - 1, -1, -1):
            rim_copy(1, partner(s, i, n_sky), s).start()

    base = base - source_term(jnp.concatenate(step, axis=0))
    on_base = against_params(base)
    for i in range(1, n_sky):
        coef_copy(i).wait_recv()

    @pl.when(jnp.logical_and(not_first, jnp.logical_not(at_high)))
    def _():
        pass_copy(0, 1).wait_recv()

    @pl.when(jnp.logical_and(not_last, jnp.logical_not(at_low)))
    def _():
        pass_copy(1, 1).wait_recv()

    @pl.when(first_t)
    def _():
        edge_all[0] = jnp.zeros(edge_all.shape[1:], F32)
        rim_all[1] = jnp.zeros(rim_all.shape[1:], F32)

    @pl.when(last_t)
    def _():
        edge_all[1] = jnp.zeros(edge_all.shape[1:], F32)
        rim_all[0] = jnp.zeros(rim_all.shape[1:], F32)

    def coef_lines(first, last):
        out = []
        for l in range(first, last):
            j, c = l // per, l % per
            line = jnp.concatenate([coef_all[h, j * k16 : (j + 1) * k16] for h in range(n_sky)], axis=1)
            ends = [jnp.where(edge_lane == l, edge_all[side], 0.0) for side in range(2)]
            out.append(jnp.concatenate([jnp.where(line_lane == c, line, 0.0)] + ends, axis=1))
        return jnp.concatenate(out, axis=0)

    inv_lines, term_lines = coef_lines(0, NAX), coef_lines(NAX, n_lines)
    inv_near = left_dot(inv_lines, near_hot)
    got = left_dot(term_lines, near_hot[:, cross : (n_near - 1) * cross])
    terms_near = [
        [
            rows_of(got[b * NAX * k16 : (b + 1) * NAX * k16, m * cross : (m + 1) * cross])
            for m in range(n_near - 2)
        ]
        for b in range(n_band)
    ]

    shape = (2 * REACH * LANES, 2 * tile)
    c, d = iota(shape, 0), iota(shape, 1)
    r, c = c // LANES, c % LANES
    spot = (c // k16) * span + jnp.where(r < REACH, r, tile + blocks + r)
    rim_fold = onehot(jnp.logical_and(c < NAX * k16, d == spot))
    rim_knot = iota((k16, LANES), 0) == iota((k16, LANES), 1) % k16

    @pl.when(not_last)
    def _():
        for i in range(n_sky):
            rim_copy(0, i, i).wait_recv()

    @pl.when(not_first)
    def _():
        for i in range(n_sky):
            rim_copy(1, i, i).wait_recv()

    rim_rows = []
    for side in (1, 0):
        total = rim_all[side, 0]
        for i in range(1, n_sky):
            total = total + rim_all[side, i]
        rim_rows = rim_rows + [total[i : i + 1] for i in range(REACH)]
    rim_cols = jnp.transpose(
        jnp.concatenate(rim_rows + [jnp.zeros((LANES - 2 * REACH, LANES), F32)], axis=0)
    )
    found = iota((LANES, 1), 0)
    found = jnp.where(found < REACH, found - REACH, found + n_blocks - REACH)
    found = jnp.where(iota((LANES, 1), 0) < 2 * REACH, found, -8 * REACH)
    grad = left_dot(rim_cols[: NAX * k16], onehot(found.astype(F32) == near_row))

    group = 2 if n_sky % 2 == 0 else 1

    def scatter(j, total):
        home = partner(s // group, j, n_sky // group) * group
        lines = jnp.concatenate([lanes_of(grads_all[home + x]) for x in range(group)], axis=1)
        hots = [hot_all[home + x] if prebuilt else sender_hot(home + x) for x in range(group)]
        return total + left_dot(lines, jnp.concatenate(hots, axis=1), NT)

    for x in range(1, group):
        grads_copy(x).wait_recv()
    grad = scatter(0, grad)

    def add_group(j, total):
        for x in range(group):
            grads_copy(j * group + x).wait_recv()
        return scatter(j, total)

    if prebuilt:
        for j in range(1, n_sky // group):
            grad = add_group(j, grad)
    else:
        grad = lax.fori_loop(1, n_sky // group, add_group, grad)

    first = grad * inv_near
    moved = smooth_near(
        [rows_of(first[:, m * cross : (m + 1) * cross]) for m in range(n_near)], terms_near
    )
    fetched = fetched + moved
    send_rhs(1, fetched, on_base)
    grads = grads_of(base, fetched)
    win_hot = onehot(window_col(n_sky + 2, -1) == block_row)
    own_col = window_col(1, s)
    own_row = jnp.concatenate([kb_all[h] for h in range(n_sky)], axis=1)
    own_hot = onehot(jnp.concatenate([own_col] * n_sky, axis=1) == own_row)
    lines = jnp.concatenate([lanes_of(grads_all[h]) for h in range(n_sky)], axis=1)
    grad_own = pick_axes(left_dot(lines, own_hot, NT), 1)
    rim_tiles = left_dot(
        jnp.concatenate([jnp.where(rim_knot, row, 0.0) for row in rim_rows], axis=1), rim_fold
    )
    grad_own = grad_own + jnp.where(at_low, rim_tiles[:, :tile], 0.0)
    grad_own = grad_own + jnp.where(at_high, rim_tiles[:, tile:], 0.0)
    rhs = wait_rhs(1)
    rhs_total = rhs_total + rhs
    grads = move_grads(grads, step_of(rhs))
    picked = pick_axes(left_dot(lanes_of(grads), win_hot, NT), n_sky + 2)
    for h in range(n_sky + 2):
        win_mine[h] = picked[:, h * tile : (h + 1) * tile]

    for i in range(n_sky - 1, 0, -1):
        win_copy(i).start()

    @pl.when(not_last)
    def _():
        low_copy(s).start()

    @pl.when(not_first)
    def _():
        high_copy(s).start()

    win_all[s] = win_mine[1 + s]
    from_low, from_high = jnp.logical_and(at_low, not_first), jnp.logical_and(at_high, not_last)

    @pl.when(jnp.logical_not(from_low))
    def _():
        win_low[...] = jnp.zeros(win_low.shape, F32)

    @pl.when(jnp.logical_not(from_high))
    def _():
        win_high[...] = jnp.zeros(win_high.shape, F32)

    full_hot = onehot(iota((n_src, n_tm * cross), 0).astype(F32) == slots_row)
    normal_all = left_dot(rhs_total, full_hot, NT)[:NPAR]
    steps = [jnp.sum(inverses[q] * normal_all, axis=0, keepdims=True) for q in range(NPAR)]
    sources_out[...] = sources[...] + jnp.concatenate(steps, axis=0)
    shape = (n_sky * LANES, tile)
    m, at = iota((n_sky * LANES, 1), 0), iota((1, tile), 1)
    i = at
    for a in range(1, NAX):
        i = i - jnp.where(at >= a * span, span, 0)
    own_place = jnp.where(at >= NAX * span, -8 * REACH, s * blocks - REACH + i).astype(F32)
    found = [
        m // LANES * blocks + m % blocks,
        iota((LANES, 1), 0) % REACH - REACH,
        iota((LANES, 1), 0) % REACH + n_blocks,
    ]
    coef_hot = jnp.concatenate([onehot(x.astype(F32) == own_place) for x in found], axis=0)
    got = left_dot(jnp.concatenate([inv_lines, term_lines], axis=0), coef_hot)
    own = [pick_axes(got[b * NAX * k16 : (b + 1) * NAX * k16], 1) for b in range(n_band + 1)]
    inv_own, terms_own = own[0], own[1:]
    shape = (knots_here, tile)
    unfold = jnp.concatenate(
        [onehot(iota(shape, 1) == (iota(shape, 0) // k16) + (span * a + REACH)) for a in range(NAX)], axis=0
    )

    for i in range(1, n_sky):
        win_copy(i).wait_recv()

    @pl.when(from_low)
    def _():
        for i in range(n_sky):
            low_copy(i).wait_recv()

    @pl.when(from_high)
    def _():
        for i in range(n_sky):
            high_copy(i).wait_recv()

    grad = grad_own
    for i in range(n_sky):
        grad = grad + (win_all[i] + win_low[i] + win_high[i])
    moved = smooth(grad, inv_own, terms_own)

    line = left_dot(moved, unfold, NT)
    for a in range(NAX):
        own = jnp.where(own_knot, line[:, a * knots_here : (a + 1) * knots_here], 0.0)
        attitude_out[a] = attitude[a] + jnp.sum(own, axis=0, keepdims=True)

    for i in range(1, n_sky):
        knots_copy(i).wait_send()
        coef_copy(i).wait_send()
        kb_copy(i).wait_send()
        grads_copy(i).wait_send()
        win_copy(i).wait_send()
    for i in range(1, n_tm):
        slots_copy(i).wait_send()
        for it in range(ITERS):
            rhs_copy(it, i).wait_send()

    @pl.when(jnp.logical_and(at_high, not_last))
    def _():
        near_copy(0).wait_send()

    @pl.when(jnp.logical_and(at_low, not_first))
    def _():
        near_copy(1).wait_send()

    @pl.when(take_low)
    def _():
        for i in range(1, n_sky):
            pass_copy(0, i).wait_send()

    @pl.when(take_high)
    def _():
        for i in range(1, n_sky):
            pass_copy(1, i).wait_send()

    @pl.when(not_first)
    def _():
        for i in range(n_sky):
            rim_copy(0, i, s).wait_send()
        high_copy(s).wait_send()

    @pl.when(not_last)
    def _():
        for i in range(n_sky):
            rim_copy(1, i, s).wait_send()
        low_copy(s).wait_send()


def finish(sources_in, attitude_in, sources_out, attitude_out):
    sources_out[...] = sources_in[...]
    attitude_out[...] = attitude_in[...]


def per_device(
    observed,
    att_partials,
    src_partials,
    src_slot,
    knot_block,
    live_count,
    sources,
    inverses,
    attitude,
    band_coef,
    extra_diag,
    band_offsets,
):
    n_sky, n_tm = lax.axis_size("sky"), lax.axis_size("tm")
    blocks = attitude.shape[2] // BLOCK_KNOTS
    cross = src_slot.shape[0]
    k16 = BLOCK_KNOTS
    tile = -(-NAX * (blocks + 2 * REACH) // LANES) * LANES
    n_tiles = -(-(1 + band_coef.shape[0]) * NAX * blocks // LANES)
    n_near = (2 * REACH + 1) * cross
    n_hot = n_sky if n_sky * n_near * cross * 2 <= HOT_CAP else 1
    vmem = pl.BlockSpec(memory_space=pltpu.VMEM)
    hbm = pl.BlockSpec(memory_space=pl.ANY)
    dma = pltpu.SemaphoreType.DMA
    results = pl.pallas_call(
        functools.partial(kernel, n_sky, n_tm),
        out_shape=(
            pltpu.VMEM(sources.shape, F32),
            pltpu.VMEM(attitude.shape, F32),
        ),
        in_specs=[hbm] * 12,
        out_specs=(vmem, vmem),
        scratch_shapes=[
            pltpu.VMEM(observed.shape, F32),
            pltpu.VMEM(att_partials.shape, BF16),
            pltpu.VMEM(src_partials.shape, BF16),
            pltpu.VMEM((1, cross), jnp.int32),
            pltpu.VMEM((1, cross), jnp.int32),
            pltpu.SMEM(live_count.shape, jnp.int32),
            pltpu.VMEM(sources.shape, F32),
            pltpu.VMEM(inverses.shape, F32),
            pltpu.VMEM(attitude.shape, F32),
            pltpu.VMEM(band_coef.shape, F32),
            pltpu.VMEM(extra_diag.shape, F32),
            pltpu.SMEM(band_offsets.shape, jnp.int32),
            dma((12,)),
            pltpu.VMEM((n_sky, k16, LANES), F32),
            pltpu.VMEM((n_sky, n_tiles * k16, LANES), F32),
            pltpu.VMEM((n_sky, 1, cross), F32),
            pltpu.VMEM((n_tm, 1, cross), F32),
            pltpu.VMEM((ITERS, n_tm, 8, cross), F32),
            pltpu.VMEM((n_sky, k16, NAX * cross), F32),
            pltpu.VMEM((2, REACH, LANES), F32),
            pltpu.VMEM((2, n_sky, REACH, LANES), F32),
            pltpu.VMEM((n_sky + 2, k16, tile), F32),
            pltpu.VMEM((n_sky, k16, tile), F32),
            pltpu.VMEM((n_sky, k16, tile), F32),
            pltpu.VMEM((n_sky, k16, tile), F32),
            pltpu.VMEM((2, k16, LANES), F32),
            pltpu.VMEM((2, k16, LANES), F32),
            pltpu.VMEM((n_hot, n_near, cross), BF16),
            dma((n_sky,)),
            dma((n_sky,)),
            dma((n_sky,)),
            dma((n_sky,)),
            dma((n_sky,)),
            dma((n_sky,)),
            dma((2,)),
            dma((2,)),
            dma((2, n_sky)),
            dma((2,)),
            dma((n_tm,)),
            dma((n_tm,)),
            dma((ITERS, n_tm)),
            dma((ITERS, n_tm)),
            dma((n_sky,)),
            dma((n_sky,)),
            dma((2, n_sky)),
            dma((2, n_sky)),
            dma((n_sky,)),
            dma((n_sky,)),
            dma((2,)),
            dma((n_sky,)),
            dma((n_sky,)),
        ],
        compiler_params=pltpu.CompilerParams(
            collective_id=0, has_side_effects=True, vmem_limit_bytes=VMEM_LIMIT
        ),
    )(
        observed,
        att_partials,
        src_partials,
        src_slot[None, :],
        knot_block[None, :],
        live_count,
        sources,
        inverses,
        attitude,
        band_coef,
        extra_diag,
        band_offsets,
    )
    return pl.pallas_call(
        finish,
        out_shape=(
            jax.ShapeDtypeStruct(sources.shape, F32),
            jax.ShapeDtypeStruct(attitude.shape, F32),
        ),
        in_specs=[vmem] * 2,
        out_specs=(vmem, vmem),
        compiler_params=pltpu.CompilerParams(vmem_limit_bytes=1 << 20),
    )(*results)


def solution(mesh):
    placed = (
        P(("sky", "tm"), None),
        P(None, ("sky", "tm"), None),
        P(None, ("sky", "tm"), None),
        P(("sky", "tm")),
        P(("sky", "tm")),
        P(("sky", "tm")),
        P(None, "sky"),
        P(None, None, "sky"),
        P(None, "tm", "sky"),
        P(None, None, "tm", "sky"),
        P(None, "tm", "sky"),
        P(),
    )
    return jax.shard_map(
        per_device,
        mesh=mesh,
        in_specs=placed,
        out_specs=(P(None, "sky"), P(None, "tm", "sky")),
        check_vma=False,
    )
```

```python
import functools

import jax
import jax.numpy as jnp
from jax import lax
from jax.experimental import pallas as pl
from jax.experimental.pallas import tpu as pltpu
from jax.sharding import PartitionSpec as P

BLOCK_KNOTS = 16
SWEEPS = 3
ITERS = 2
NPAR = 5
NAX = 3
LANES = 128
REACH = 2
HOT_CAP = 4 << 20
VMEM_LIMIT = 61960 << 10
MESH = pl.DeviceIdType.MESH
F32 = jnp.float32
BF16 = jnp.bfloat16

NN = (((1,), (0,)), ((), ()))
NT = (((1,), (1,)), ((), ()))


def iota(shape, dim):
    return lax.broadcasted_iota(jnp.int32, shape, dim)


def onehot(mask):
    return jnp.where(mask, 1.0, 0.0).astype(BF16)


def parts(x):
    high = x.astype(BF16)
    return high, (x - high.astype(F32)).astype(BF16)


def mm(a, b, dims=NN):
    return lax.dot_general(a, b, dims, preferred_element_type=F32)


def left_dot(x, hot, dims=NN):
    n = x.shape[0]
    out = mm(jnp.concatenate(parts(x), axis=0), hot, dims)
    return out[:n] + out[n:]


def spline_at(row, knot, rows):
    moment = 1.5 + (BLOCK_KNOTS - 3) * (row.astype(F32) + 0.5) / rows
    dist = jnp.abs(moment - knot.astype(F32))
    inner = 2.0 / 3.0 - dist * dist + 0.5 * dist * dist * dist
    rest = 2.0 - dist
    outer = rest * rest * rest / 6.0
    return jnp.where(dist < 1.0, inner, jnp.where(dist < 2.0, outer, 0.0))


def partner(me, i, n):
    if n & (n - 1):
        return lax.rem(me + i, n)
    out, bit = me, 1
    while bit < n:
        out = out + ((i // bit) % 2) * bit * (1 - 2 * ((me // bit) % 2))
        bit *= 2
    return out


def kernel(
    n_sky,
    n_tm,
    observed_in,
    att_partials_in,
    src_partials_in,
    src_slot_in,
    knot_block_in,
    live_count_in,
    sources_in,
    inverses_in,
    attitude_in,
    band_coef_in,
    extra_diag_in,
    band_offsets_in,
    sources_out,
    attitude_out,
    observed,
    att_partials,
    src_partials,
    src_slot,
    knot_block,
    live_count,
    sources,
    inverses,
    attitude,
    band_coef,
    extra_diag,
    band_offsets,
    input_sem,
    knots_all,
    coef_all,
    kb_all,
    slots_all,
    rhs_all,
    grads_all,
    rim_mine,
    rim_all,
    win_mine,
    win_all,
    win_low,
    win_high,
    near_mine,
    edge_all,
    hot_all,
    knots_send,
    knots_recv,
    coef_send,
    coef_recv,
    kb_send,
    kb_recv,
    near_send,
    near_recv,
    pass_send,
    pass_recv,
    slots_send,
    slots_recv,
    rhs_send,
    rhs_recv,
    grads_send,
    grads_recv,
    rim_send,
    rim_recv,
    win_send,
    win_recv,
    far_send,
    low_recv,
    high_recv,
):
    s = lax.axis_index("sky")
    t = lax.axis_index("tm")
    cross, rows = observed.shape
    knots_here = attitude.shape[2]
    blocks = knots_here // BLOCK_KNOTS
    span = blocks + 2 * REACH
    n_blocks = n_sky * blocks
    n_src = sources.shape[1]
    n_band = band_coef.shape[0]
    tile = win_all.shape[2]
    k16 = BLOCK_KNOTS
    per = LANES // blocks
    n_lines = (1 + n_band) * NAX
    n_near = 2 * REACH + 1

    first_t, last_t = t == 0, t == n_tm - 1
    at_low, at_high = s == 0, s == n_sky - 1
    not_first, not_last = t > 0, t < n_tm - 1
    t_up, t_down = jnp.minimum(t + 1, n_tm - 1), jnp.maximum(t - 1, 0)

    barrier = pltpu.get_barrier_semaphore()
    for i in range(n_sky - 1, 0, -1):
        pl.semaphore_signal(barrier, inc=1, device_id=(partner(s, i, n_sky), t), device_id_type=MESH)
    for i in range(n_tm - 1, 0, -1):
        pl.semaphore_signal(barrier, inc=1, device_id=(s, partner(t, i, n_tm)), device_id_type=MESH)

    pairs = (
        (attitude_in, attitude),
        (band_coef_in, band_coef),
        (extra_diag_in, extra_diag),
        (src_slot_in, src_slot),
        (knot_block_in, knot_block),
        (src_partials_in, src_partials),
        (att_partials_in, att_partials),
        (inverses_in, inverses),
        (sources_in, sources),
        (observed_in, observed),
        (live_count_in, live_count),
        (band_offsets_in, band_offsets),
    )
    loads = [
        pltpu.make_async_copy(source, place, input_sem.at[i])
        for i, (source, place) in enumerate(pairs)
    ]
    for load in loads:
        load.start()

    def remote(src, dst, send, recv, to):
        return pltpu.make_async_remote_copy(
            src_ref=src, dst_ref=dst, send_sem=send, recv_sem=recv, device_id=to, device_id_type=MESH
        )

    def to_sky(i):
        return (partner(s, i, n_sky), t)

    def to_tm(i):
        return (s, partner(t, i, n_tm))

    def knots_copy(i):
        return remote(knots_all.at[s], knots_all.at[s], knots_send.at[i], knots_recv.at[i], to_sky(i))

    def coef_copy(i):
        return remote(coef_all.at[s], coef_all.at[s], coef_send.at[i], coef_recv.at[i], to_sky(i))

    def kb_copy(i):
        return remote(kb_all.at[s], kb_all.at[s], kb_send.at[i], kb_recv.at[i], to_sky(i))

    def near_copy(side):
        to = (s, t_up if side == 0 else t_down)
        return remote(near_mine.at[side], edge_all.at[side], near_send.at[side], near_recv.at[side], to)

    def pass_copy(side, i):
        return remote(edge_all.at[side], edge_all.at[side], pass_send.at[side, i], pass_recv.at[side], to_sky(i))

    def slots_copy(i):
        return remote(slots_all.at[t], slots_all.at[t], slots_send.at[i], slots_recv.at[i], to_tm(i))

    def rhs_copy(it, i):
        return remote(rhs_all.at[it, t], rhs_all.at[it, t], rhs_send.at[it, i], rhs_recv.at[it, i], to_tm(i))

    def grads_copy(i):
        return remote(grads_all.at[s], grads_all.at[s], grads_send.at[i], grads_recv.at[i], to_sky(i))

    def rim_copy(side, to_s, slot):
        to = (to_s, t_down if side == 0 else t_up)
        return remote(rim_mine.at[side], rim_all.at[side, slot], rim_send.at[side, to_s], rim_recv.at[side, slot], to)

    def win_copy(i):
        to = to_sky(i)
        return remote(win_mine.at[1 + to[0]], win_all.at[s], win_send.at[i], win_recv.at[i], to)

    def low_copy(slot):
        return remote(win_mine.at[n_sky + 1], win_low.at[slot], far_send.at[0], low_recv.at[slot], (0, t_up))

    def high_copy(slot):
        return remote(win_mine.at[0], win_high.at[slot], far_send.at[1], high_recv.at[slot], (n_sky - 1, t_down))

    for load in loads[:5]:
        load.wait()
    own_knot = iota((k16, knots_here), 0) == iota((k16, knots_here), 1) % k16
    shape = (knots_here, LANES)
    fold = jnp.concatenate(
        [onehot(iota(shape, 1) == iota(shape, 0) // k16 + blocks * c) for c in range(per)], axis=0
    )

    def spread(lines):
        lines = lines + [jnp.zeros((1, knots_here), F32)] * (per - len(lines))
        return jnp.concatenate([jnp.where(own_knot, line, 0.0) for line in lines], axis=1)

    knots_all[s] = left_dot(spread([attitude[a] for a in range(NAX)]), fold)
    slot_row = src_slot[...].astype(F32)
    block_row = knot_block[...].astype(F32)
    slots_all[t] = slot_row
    kb_all[s] = block_row
    bands = [[band_coef[b, a] for a in range(NAX)] for b in range(n_band)]
    inv_diag = []
    for a in range(NAX):
        band_sum = bands[0][a]
        for b in range(1, n_band):
            band_sum = band_sum + bands[b][a]
        inv_diag.append(1.0 / (extra_diag[a] + 2.0 * band_sum))
    lines = inv_diag + [bands[b][a] * inv_diag[a] for b in range(n_band) for a in range(NAX)]
    coef = left_dot(
        jnp.concatenate([spread(lines[c : c + per]) for c in range(0, n_lines, per)], axis=0), fold
    )
    coef_all[s] = coef
    edge_lane = iota((k16, LANES), 1) // REACH
    for side in range(2):
        edge = jnp.zeros((k16, LANES), F32)
        for l in range(n_lines):
            j, c = l // per, l % per
            begin = c * blocks + (blocks - REACH if side == 0 else 0)
            moved = pltpu.roll(coef[j * k16 : (j + 1) * k16], (REACH * l - begin) % LANES, 1)
            edge = jnp.where(edge_lane == l, moved, edge)
        near_mine[side] = edge

    pl.semaphore_wait(barrier, (n_sky - 1) + (n_tm - 1))
    for i in range(n_sky - 1, 0, -1):
        knots_copy(i).start()
    for i in range(n_tm - 1, 0, -1):
        slots_copy(i).start()
    take_low, take_high = jnp.logical_and(at_high, not_first), jnp.logical_and(at_low, not_last)

    @pl.when(jnp.logical_and(at_high, not_last))
    def _():
        near_copy(0).start()

    @pl.when(jnp.logical_and(at_low, not_first))
    def _():
        near_copy(1).start()

    for i in range(n_sky - 1, 0, -1):
        kb_copy(i).start()
    for i in range(n_sky - 1, 0, -1):
        coef_copy(i).start()

    for load in loads[5:]:
        load.wait()
    lane = iota((1, cross), 1)
    live = lane < live_count[0]

    shape = (n_src, cross)
    src_hot = onehot(iota(shape, 0).astype(F32) == slot_row)
    gap_rows = jnp.zeros((8 - NPAR, n_src), F32)
    src_list = [x for q in range(NPAR) for x in (inverses[q], gap_rows)]
    gathered = left_dot(jnp.concatenate(src_list + [sources[...], gap_rows], axis=0), src_hot)

    eye = onehot(iota((rows, rows), 0) == iota((rows, rows), 1))
    par = [mm(eye, src_partials[p], NT) for p in range(NPAR)]
    att = [mm(eye, att_partials[a], NT) for a in range(NAX)]

    def source_term(values):
        total = par[0] * values[0:1]
        for p in range(1, NPAR):
            total = total + par[p] * values[p : p + 1]
        return total

    base = jnp.transpose(observed[...]) - source_term(gathered[NPAR * 8 :])

    shape = (k16, 2 * rows)
    high, low = parts(spline_at(iota(shape, 1) % rows, iota(shape, 0), rows))
    low = jnp.where(iota(shape, 1) < rows, low.astype(F32), 0.0).astype(BF16)
    back = jnp.concatenate([high, low], axis=0)
    shape = (rows, 3 * k16)
    high, low = parts(spline_at(iota(shape, 0), iota(shape, 1) % k16, rows))
    look = jnp.where(iota(shape, 1) < 2 * k16, high.astype(F32), low.astype(F32)).astype(BF16)

    def back_dot(value):
        spread = jnp.concatenate([x * value for x in att], axis=1)
        out = mm(back, jnp.concatenate(parts(spread), axis=0))
        return out[:k16] + out[k16:]

    def look_dot(knots):
        high, low = parts(knots)
        return mm(look, jnp.concatenate([high, low, high], axis=0))

    cross_terms = [back_dot(par[q]) for q in range(NPAR)]

    def against_params(value):
        return jnp.concatenate(
            [jnp.sum(par[p] * value, axis=0, keepdims=True) for p in range(NPAR)]
            + [jnp.zeros((8 - NPAR, cross), F32)],
            axis=0,
        )

    on_base = against_params(base)

    near_row = jnp.concatenate([block_row + (m - REACH) for m in range(n_near)], axis=1)
    shape = (n_sky * LANES, n_near * cross)
    found = iota((n_sky * LANES, 1), 0)
    found = found // LANES * blocks + found % blocks
    near_hot = onehot(found.astype(F32) == near_row)
    found = iota((LANES, 1), 0) % REACH
    low_hot = onehot((found - REACH).astype(F32) == near_row)
    high_hot = onehot((found + n_blocks).astype(F32) == near_row)
    near_hot = jnp.concatenate([near_hot, low_hot, high_hot], axis=0)
    mid = slice(REACH * cross, (REACH + 1) * cross)

    def window_col(count, first):
        m = iota((count * tile, LANES), 0)
        h, at = m // tile + first, m % tile
        i = at
        for a in range(1, NAX):
            i = i - jnp.where(at >= a * span, span, 0)
        return jnp.where(at >= NAX * span, -1, h * blocks - REACH + i).astype(F32)

    line_lane = iota((k16, n_sky * LANES), 1) % LANES // blocks

    def lanes_of(tiles):
        return jnp.concatenate([tiles[:, a * cross : (a + 1) * cross] for a in range(NAX)], axis=0)

    def rows_of(lines):
        return jnp.concatenate([lines[a * k16 : (a + 1) * k16] for a in range(NAX)], axis=1)

    def pick_axes(lines, count):
        lane = iota((k16, count * tile), 1) % tile
        picked = lines[(NAX - 1) * k16 :]
        for a in range(NAX - 2, -1, -1):
            picked = jnp.where(lane < (a + 1) * span, lines[a * k16 : (a + 1) * k16], picked)
        return picked

    for i in range(1, n_tm):
        slots_copy(i).wait_recv()
    slots_row = jnp.concatenate([slots_all[i] for i in range(n_tm)], axis=1)
    slot_col = jnp.transpose(jnp.broadcast_to(slot_row, (LANES, cross)))[:, :1]
    same_source = onehot(slot_col == slots_row)

    @pl.when(take_low)
    def _():
        near_copy(0).wait_recv()
        for i in range(n_sky - 1, 0, -1):
            pass_copy(0, i).start()

    @pl.when(take_high)
    def _():
        near_copy(1).wait_recv()
        for i in range(n_sky - 1, 0, -1):
            pass_copy(1, i).start()

    def shift_rows(outs, ins):
        shape = (outs * n_band * k16, ins * k16)
        c, d = iota(shape, 0), iota(shape, 1)
        m, b = c // (n_band * k16), c // k16 % n_band
        gap = jnp.abs(d - (m + (ins - outs) // 2) * k16 - c % k16)
        offset = jnp.zeros(shape, jnp.int32)
        for i in range(n_band):
            offset = jnp.where(b == i, band_offsets[i], offset)
        hot = onehot(gap == offset)
        return jnp.concatenate([hot, hot], axis=1)

    shifts = [shift_rows(n_near - 2 * i, n_near - 2 * i + 2) for i in range(1, SWEEPS)]

    def back_rows(outs, ins):
        shape = (ins * k16, outs * n_band * k16)
        c, d = iota(shape, 0), iota(shape, 1)
        m, b = d // (n_band * k16), d // k16 % n_band
        gap = jnp.abs(c - (m + (ins - outs) // 2) * k16 - d % k16)
        offset = jnp.zeros(shape, jnp.int32)
        for i in range(n_band):
            offset = jnp.where(b == i, band_offsets[i], offset)
        hot = onehot(gap == offset)
        return jnp.concatenate([hot, hot], axis=1)

    shifts_back = [back_rows(n_near - 2 * i, n_near - 2 * i + 2) for i in range(1, SWEEPS)]

    def smooth_back(value, inv, terms):
        total = [None] * n_near
        total[REACH] = value
        slots = [value]
        for i in range(SWEEPS - 1, 0, -1):
            spread = [
                terms[b][m + i - 1] * slots[m] for m in range(n_near - 2 * i) for b in range(n_band)
            ]
            out = mm(shifts_back[i - 1], jnp.concatenate(parts(jnp.concatenate(spread, axis=0)), axis=0))
            slots = [out[m * k16 : (m + 1) * k16] for m in range(n_near - 2 * i + 2)]
            for m, slot in enumerate(slots):
                at = m + i - 1
                total[at] = slot if total[at] is None else total[at] + slot
        return [inv[m] * total[m] for m in range(n_near)]

    def smooth_near(first, terms):
        delta = first
        for i in range(1, SWEEPS):
            sums = mm(shifts[i - 1], jnp.concatenate(parts(jnp.concatenate(delta, axis=0)), axis=0))
            delta = []
            for m in range(n_near - 2 * i):
                at = m + i
                total = first[at]
                for b in range(n_band):
                    row = (m * n_band + b) * k16
                    total = total + terms[b][at - 1] * sums[row : row + k16]
                delta.append(total)
        return delta[0]

    def smooth(grad, inv, terms):
        first = grad * inv
        delta = first
        for sweep in range(SWEEPS - 1):
            near = jnp.concatenate([pltpu.roll(delta, 1, 1), delta, pltpu.roll(delta, tile - 1, 1)], axis=0)
            sums = mm(shifts[-1], jnp.concatenate(parts(near), axis=0))
            delta = first
            for b in range(n_band):
                delta = delta + terms[b] * sums[b * k16 : (b + 1) * k16]
        return delta

    for i in range(1, n_sky):
        knots_copy(i).wait_recv()
    knots = jnp.concatenate([knots_all[h] for h in range(n_sky)], axis=1)
    knots = jnp.concatenate([jnp.where(line_lane == a, knots, 0.0) for a in range(NAX)], axis=0)
    fetched = rows_of(left_dot(knots, near_hot[: n_sky * LANES, mid]))

    def rhs_term(fetched):
        out = []
        for q in range(NPAR):
            term = jnp.sum(fetched * cross_terms[q], axis=0, keepdims=True)
            total = term[:, :cross]
            for a in range(1, NAX):
                total = total + term[:, a * cross : (a + 1) * cross]
            out.append(total)
        out.append(jnp.zeros((8 - NPAR, cross), F32))
        return jnp.concatenate(out, axis=0)

    def send_rhs(it, rhs):
        rhs_all[it, t] = jnp.where(live, rhs, 0.0)
        for i in range(n_tm - 1, 0, -1):
            rhs_copy(it, i).start()

    def grads_of(base, fetched):
        seen = look_dot(fetched)
        resid = base
        for a in range(NAX):
            resid = resid - att[a] * seen[:, a * cross : (a + 1) * cross]
        return back_dot(jnp.where(live, resid, 0.0))

    def wait_rhs(it):
        for i in range(1, n_tm):
            rhs_copy(it, i).wait_recv()
        return jnp.concatenate([rhs_all[it, i] for i in range(n_tm)], axis=1)

    live_all = jnp.concatenate([live] * NAX, axis=1)

    def step_of(rhs):
        normal = left_dot(rhs, same_source, NT)
        return [
            jnp.sum(gathered[q * 8 : (q + 1) * 8] * normal, axis=0, keepdims=True)
            for q in range(NPAR)
        ]

    def move_grads(grads, step):
        total = jnp.concatenate([step[0]] * NAX, axis=1) * cross_terms[0]
        for q in range(1, NPAR):
            total = total + jnp.concatenate([step[q]] * NAX, axis=1) * cross_terms[q]
        return grads - jnp.where(live_all, total, 0.0)

    send_rhs(0, on_base - rhs_term(fetched))
    grads = grads_of(base, fetched)

    for i in range(1, n_sky):
        kb_copy(i).wait_recv()

    prebuilt = hot_all.shape[0] == n_sky

    block_col = jnp.transpose(jnp.broadcast_to(block_row, (LANES, cross)))
    near_col = jnp.concatenate([block_col + (m - REACH) for m in range(n_near)], axis=0)

    def sender_hot(h):
        return onehot(near_col == kb_all[h])

    if prebuilt:
        for h in range(n_sky):
            hot_all[h] = sender_hot(h)

    rim_row = iota((k16, cross), 0)
    rim_block = jnp.where(rim_row < 8, rim_row, n_blocks - REACH - 8 + rim_row)
    rim_hot = onehot(
        jnp.logical_and(rim_row % 8 < REACH, rim_block.astype(F32) == block_row)
    )

    rhs = wait_rhs(0)
    rhs_total = rhs
    step = step_of(rhs)
    grads = move_grads(grads, step)
    grads_all[s] = grads
    for i in range(n_sky - 1, n_sky // 2 - 1, -1):
        grads_copy(i).start()

    high, low = parts(lanes_of(grads))
    gap_rows = jnp.zeros((LANES - NAX * k16, cross), BF16)
    rims = mm(rim_hot, jnp.concatenate([high, gap_rows], axis=0), NT) + mm(
        rim_hot, jnp.concatenate([low, gap_rows], axis=0), NT
    )
    rim_mine[0] = rims[:REACH]
    rim_mine[1] = rims[8 : 8 + REACH]

    @pl.when(not_first)
    def _():
        for i in range(n_sky - 1, -1, -1):
            rim_copy(0, partner(s, i, n_sky), s).start()

    @pl.when(not_last)
    def _():
        for i in range(n_sky - 1, -1, -1):
            rim_copy(1, partner(s, i, n_sky), s).start()

    for i in range(n_sky // 2 - 1, 0, -1):
        grads_copy(i).start()

    base = base - source_term(jnp.concatenate(step, axis=0))
    on_base = against_params(base) - rhs_term(fetched)
    for i in range(1, n_sky):
        coef_copy(i).wait_recv()

    @pl.when(jnp.logical_and(not_first, jnp.logical_not(at_high)))
    def _():
        pass_copy(0, 1).wait_recv()

    @pl.when(jnp.logical_and(not_last, jnp.logical_not(at_low)))
    def _():
        pass_copy(1, 1).wait_recv()

    @pl.when(first_t)
    def _():
        edge_all[0] = jnp.zeros(edge_all.shape[1:], F32)
        rim_all[1] = jnp.zeros(rim_all.shape[1:], F32)

    @pl.when(last_t)
    def _():
        edge_all[1] = jnp.zeros(edge_all.shape[1:], F32)
        rim_all[0] = jnp.zeros(rim_all.shape[1:], F32)

    def coef_lines(first, last):
        out = []
        for l in range(first, last):
            j, c = l // per, l % per
            line = jnp.concatenate([coef_all[h, j * k16 : (j + 1) * k16] for h in range(n_sky)], axis=1)
            ends = [jnp.where(edge_lane == l, edge_all[side], 0.0) for side in range(2)]
            out.append(jnp.concatenate([jnp.where(line_lane == c, line, 0.0)] + ends, axis=1))
        return jnp.concatenate(out, axis=0)

    inv_lines, term_lines = coef_lines(0, NAX), coef_lines(NAX, n_lines)
    inv_near = left_dot(inv_lines, near_hot)
    got = left_dot(term_lines, near_hot[:, cross : (n_near - 1) * cross])
    terms_near = [
        [
            rows_of(got[b * NAX * k16 : (b + 1) * NAX * k16, m * cross : (m + 1) * cross])
            for m in range(n_near - 2)
        ]
        for b in range(n_band)
    ]

    inv_slots = [rows_of(inv_near[:, m * cross : (m + 1) * cross]) for m in range(n_near)]
    weights = smooth_back(
        jnp.concatenate(cross_terms, axis=1),
        [jnp.concatenate([x] * NPAR, axis=1) for x in inv_slots],
        [[jnp.concatenate([x] * NPAR, axis=1) for x in row] for row in terms_near],
    )

    shape = (2 * REACH * LANES, 2 * tile)
    c, d = iota(shape, 0), iota(shape, 1)
    r, c = c // LANES, c % LANES
    spot = (c // k16) * span + jnp.where(r < REACH, r, tile + blocks + r)
    rim_fold = onehot(jnp.logical_and(c < NAX * k16, d == spot))
    rim_knot = iota((k16, LANES), 0) == iota((k16, LANES), 1) % k16

    group = 2 if n_sky % 2 == 0 else 1

    def scatter(j, total):
        home = partner(s // group, j, n_sky // group) * group
        lines = jnp.concatenate([lanes_of(grads_all[home + x]) for x in range(group)], axis=1)
        hots = [hot_all[home + x] if prebuilt else sender_hot(home + x) for x in range(group)]
        return total + left_dot(lines, jnp.concatenate(hots, axis=1), NT)

    for x in range(1, group):
        grads_copy(x).wait_recv()
    grad = scatter(0, jnp.zeros((NAX * k16, n_near * cross), F32))

    def add_group(j, total):
        for x in range(group):
            grads_copy(j * group + x).wait_recv()
        return scatter(j, total)

    if prebuilt:
        for j in range(1, n_sky // group - 1):
            grad = add_group(j, grad)
    else:
        grad = lax.fori_loop(1, n_sky // group - 1, add_group, grad)

    @pl.when(not_last)
    def _():
        for i in range(n_sky):
            rim_copy(0, i, i).wait_recv()

    @pl.when(not_first)
    def _():
        for i in range(n_sky):
            rim_copy(1, i, i).wait_recv()

    rim_rows = []
    for side in (1, 0):
        total = rim_all[side, 0]
        for i in range(1, n_sky):
            total = total + rim_all[side, i]
        rim_rows = rim_rows + [total[i : i + 1] for i in range(REACH)]
    rim_cols = jnp.transpose(
        jnp.concatenate(rim_rows + [jnp.zeros((LANES - 2 * REACH, LANES), F32)], axis=0)
    )
    found = iota((LANES, 1), 0)
    found = jnp.where(found < REACH, found - REACH, found + n_blocks - REACH)
    found = jnp.where(iota((LANES, 1), 0) < 2 * REACH, found, -8 * REACH)
    grad = grad + left_dot(rim_cols[: NAX * k16], onehot(found.astype(F32) == near_row))

    grad = add_group(n_sky // group - 1, grad)


    slots = [rows_of(grad[:, m * cross : (m + 1) * cross]) for m in range(n_near)]
    out = []
    for q in range(NPAR):
        total = None
        for a in range(NAX):
            at = (q * NAX + a) * cross
            for m in range(n_near):
                term = weights[m][:, at : at + cross] * slots[m][:, a * cross : (a + 1) * cross]
                total = term if total is None else total + term
        out.append(jnp.sum(total, axis=0, keepdims=True))
    out.append(jnp.zeros((8 - NPAR, cross), F32))
    send_rhs(1, on_base - jnp.concatenate(out, axis=0))
    fetched = fetched + smooth_near([slots[m] * inv_slots[m] for m in range(n_near)], terms_near)
    grads = grads_of(base, fetched)
    win_hot = onehot(window_col(n_sky + 2, -1) == block_row)
    own_col = window_col(1, s)
    own_row = jnp.concatenate([kb_all[h] for h in range(n_sky)], axis=1)
    own_hot = onehot(jnp.concatenate([own_col] * n_sky, axis=1) == own_row)
    lines = jnp.concatenate([lanes_of(grads_all[h]) for h in range(n_sky)], axis=1)
    grad_own = pick_axes(left_dot(lines, own_hot, NT), 1)
    rim_tiles = left_dot(
        jnp.concatenate([jnp.where(rim_knot, row, 0.0) for row in rim_rows], axis=1), rim_fold
    )
    grad_own = grad_own + jnp.where(at_low, rim_tiles[:, :tile], 0.0)
    grad_own = grad_own + jnp.where(at_high, rim_tiles[:, tile:], 0.0)
    rhs = wait_rhs(1)
    rhs_total = rhs_total + rhs
    grads = move_grads(grads, step_of(rhs))
    picked = pick_axes(left_dot(lanes_of(grads), win_hot, NT), n_sky + 2)
    for h in range(n_sky + 2):
        win_mine[h] = picked[:, h * tile : (h + 1) * tile]

    for i in range(n_sky - 1, 0, -1):
        win_copy(i).start()

    @pl.when(not_last)
    def _():
        low_copy(s).start()

    @pl.when(not_first)
    def _():
        high_copy(s).start()

    win_all[s] = win_mine[1 + s]
    from_low, from_high = jnp.logical_and(at_low, not_first), jnp.logical_and(at_high, not_last)

    @pl.when(jnp.logical_not(from_low))
    def _():
        win_low[...] = jnp.zeros(win_low.shape, F32)

    @pl.when(jnp.logical_not(from_high))
    def _():
        win_high[...] = jnp.zeros(win_high.shape, F32)

    full_hot = onehot(iota((n_src, n_tm * cross), 0).astype(F32) == slots_row)
    normal_all = left_dot(rhs_total, full_hot, NT)[:NPAR]
    steps = [jnp.sum(inverses[q] * normal_all, axis=0, keepdims=True) for q in range(NPAR)]
    sources_out[...] = sources[...] + jnp.concatenate(steps, axis=0)
    shape = (n_sky * LANES, tile)
    m, at = iota((n_sky * LANES, 1), 0), iota((1, tile), 1)
    i = at
    for a in range(1, NAX):
        i = i - jnp.where(at >= a * span, span, 0)
    own_place = jnp.where(at >= NAX * span, -8 * REACH, s * blocks - REACH + i).astype(F32)
    found = [
        m // LANES * blocks + m % blocks,
        iota((LANES, 1), 0) % REACH - REACH,
        iota((LANES, 1), 0) % REACH + n_blocks,
    ]
    coef_hot = jnp.concatenate([onehot(x.astype(F32) == own_place) for x in found], axis=0)
    got = left_dot(jnp.concatenate([inv_lines, term_lines], axis=0), coef_hot)
    own = [pick_axes(got[b * NAX * k16 : (b + 1) * NAX * k16], 1) for b in range(n_band + 1)]
    inv_own, terms_own = own[0], own[1:]
    shape = (knots_here, tile)
    unfold = jnp.concatenate(
        [onehot(iota(shape, 1) == (iota(shape, 0) // k16) + (span * a + REACH)) for a in range(NAX)], axis=0
    )

    for i in range(1, n_sky):
        knots_copy(i).wait_send()
        coef_copy(i).wait_send()
        kb_copy(i).wait_send()
        grads_copy(i).wait_send()
    for i in range(1, n_tm):
        slots_copy(i).wait_send()
        for it in range(ITERS):
            rhs_copy(it, i).wait_send()

    @pl.when(jnp.logical_and(at_high, not_last))
    def _():
        near_copy(0).wait_send()

    @pl.when(jnp.logical_and(at_low, not_first))
    def _():
        near_copy(1).wait_send()

    @pl.when(take_low)
    def _():
        for i in range(1, n_sky):
            pass_copy(0, i).wait_send()

    @pl.when(take_high)
    def _():
        for i in range(1, n_sky):
            pass_copy(1, i).wait_send()

    @pl.when(not_first)
    def _():
        for i in range(n_sky):
            rim_copy(0, i, s).wait_send()

    @pl.when(not_last)
    def _():
        for i in range(n_sky):
            rim_copy(1, i, s).wait_send()

    for i in range(1, n_sky):
        win_copy(i).wait_recv()

    @pl.when(from_low)
    def _():
        for i in range(n_sky):
            low_copy(i).wait_recv()

    @pl.when(from_high)
    def _():
        for i in range(n_sky):
            high_copy(i).wait_recv()

    grad = grad_own
    for i in range(n_sky):
        grad = grad + (win_all[i] + win_low[i] + win_high[i])
    moved = smooth(grad, inv_own, terms_own)

    line = left_dot(moved, unfold, NT)
    for a in range(NAX):
        own = jnp.where(own_knot, line[:, a * knots_here : (a + 1) * knots_here], 0.0)
        attitude_out[a] = attitude[a] + jnp.sum(own, axis=0, keepdims=True)

    for i in range(1, n_sky):
        win_copy(i).wait_send()

    @pl.when(not_first)
    def _():
        high_copy(s).wait_send()

    @pl.when(not_last)
    def _():
        low_copy(s).wait_send()


def finish(sources_in, attitude_in, sources_out, attitude_out):
    sources_out[...] = sources_in[...]
    attitude_out[...] = attitude_in[...]


def per_device(
    observed,
    att_partials,
    src_partials,
    src_slot,
    knot_block,
    live_count,
    sources,
    inverses,
    attitude,
    band_coef,
    extra_diag,
    band_offsets,
):
    n_sky, n_tm = lax.axis_size("sky"), lax.axis_size("tm")
    blocks = attitude.shape[2] // BLOCK_KNOTS
    cross = src_slot.shape[0]
    k16 = BLOCK_KNOTS
    tile = -(-NAX * (blocks + 2 * REACH) // LANES) * LANES
    n_tiles = -(-(1 + band_coef.shape[0]) * NAX * blocks // LANES)
    n_near = (2 * REACH + 1) * cross
    n_hot = n_sky if n_sky * n_near * cross * 2 <= HOT_CAP else 1
    vmem = pl.BlockSpec(memory_space=pltpu.VMEM)
    hbm = pl.BlockSpec(memory_space=pl.ANY)
    dma = pltpu.SemaphoreType.DMA
    results = pl.pallas_call(
        functools.partial(kernel, n_sky, n_tm),
        out_shape=(
            pltpu.VMEM(sources.shape, F32),
            pltpu.VMEM(attitude.shape, F32),
        ),
        in_specs=[hbm] * 12,
        out_specs=(vmem, vmem),
        scratch_shapes=[
            pltpu.VMEM(observed.shape, F32),
            pltpu.VMEM(att_partials.shape, BF16),
            pltpu.VMEM(src_partials.shape, BF16),
            pltpu.VMEM((1, cross), jnp.int32),
            pltpu.VMEM((1, cross), jnp.int32),
            pltpu.SMEM(live_count.shape, jnp.int32),
            pltpu.VMEM(sources.shape, F32),
            pltpu.VMEM(inverses.shape, F32),
            pltpu.VMEM(attitude.shape, F32),
            pltpu.VMEM(band_coef.shape, F32),
            pltpu.VMEM(extra_diag.shape, F32),
            pltpu.SMEM(band_offsets.shape, jnp.int32),
            dma((12,)),
            pltpu.VMEM((n_sky, k16, LANES), F32),
            pltpu.VMEM((n_sky, n_tiles * k16, LANES), F32),
            pltpu.VMEM((n_sky, 1, cross), F32),
            pltpu.VMEM((n_tm, 1, cross), F32),
            pltpu.VMEM((ITERS, n_tm, 8, cross), F32),
            pltpu.VMEM((n_sky, k16, NAX * cross), F32),
            pltpu.VMEM((2, REACH, LANES), F32),
            pltpu.VMEM((2, n_sky, REACH, LANES), F32),
            pltpu.VMEM((n_sky + 2, k16, tile), F32),
            pltpu.VMEM((n_sky, k16, tile), F32),
            pltpu.VMEM((n_sky, k16, tile), F32),
            pltpu.VMEM((n_sky, k16, tile), F32),
            pltpu.VMEM((2, k16, LANES), F32),
            pltpu.VMEM((2, k16, LANES), F32),
            pltpu.VMEM((n_hot, n_near, cross), BF16),
            dma((n_sky,)),
            dma((n_sky,)),
            dma((n_sky,)),
            dma((n_sky,)),
            dma((n_sky,)),
            dma((n_sky,)),
            dma((2,)),
            dma((2,)),
            dma((2, n_sky)),
            dma((2,)),
            dma((n_tm,)),
            dma((n_tm,)),
            dma((ITERS, n_tm)),
            dma((ITERS, n_tm)),
            dma((n_sky,)),
            dma((n_sky,)),
            dma((2, n_sky)),
            dma((2, n_sky)),
            dma((n_sky,)),
            dma((n_sky,)),
            dma((2,)),
            dma((n_sky,)),
            dma((n_sky,)),
        ],
        compiler_params=pltpu.CompilerParams(
            collective_id=0, has_side_effects=True, vmem_limit_bytes=VMEM_LIMIT
        ),
    )(
        observed,
        att_partials,
        src_partials,
        src_slot[None, :],
        knot_block[None, :],
        live_count,
        sources,
        inverses,
        attitude,
        band_coef,
        extra_diag,
        band_offsets,
    )
    return pl.pallas_call(
        finish,
        out_shape=(
            jax.ShapeDtypeStruct(sources.shape, F32),
            jax.ShapeDtypeStruct(attitude.shape, F32),
        ),
        in_specs=[vmem] * 2,
        out_specs=(vmem, vmem),
        compiler_params=pltpu.CompilerParams(vmem_limit_bytes=1 << 20),
    )(*results)


def solution(mesh):
    placed = (
        P(("sky", "tm"), None),
        P(None, ("sky", "tm"), None),
        P(None, ("sky", "tm"), None),
        P(("sky", "tm")),
        P(("sky", "tm")),
        P(("sky", "tm")),
        P(None, "sky"),
        P(None, None, "sky"),
        P(None, "tm", "sky"),
        P(None, None, "tm", "sky"),
        P(None, "tm", "sky"),
        P(),
    )
    return jax.shard_map(
        per_device,
        mesh=mesh,
        in_specs=placed,
        out_specs=(P(None, "sky"), P(None, "tm", "sky")),
        check_vma=False,
    )
```

```python
import functools

import jax
import jax.numpy as jnp
from jax import lax
from jax.experimental import pallas as pl
from jax.experimental.pallas import tpu as pltpu
from jax.sharding import PartitionSpec as P

BLOCK_KNOTS = 16
SWEEPS = 3
ITERS = 2
NPAR = 5
NAX = 3
LANES = 128
REACH = 2
HOT_CAP = 4 << 20
VMEM_LIMIT = 61960 << 10
MESH = pl.DeviceIdType.MESH
F32 = jnp.float32
BF16 = jnp.bfloat16

NN = (((1,), (0,)), ((), ()))
NT = (((1,), (1,)), ((), ()))


def iota(shape, dim):
    return lax.broadcasted_iota(jnp.int32, shape, dim)


def onehot(mask):
    return jnp.where(mask, 1.0, 0.0).astype(BF16)


def parts(x):
    high = x.astype(BF16)
    return high, (x - high.astype(F32)).astype(BF16)


def mm(a, b, dims=NN):
    return lax.dot_general(a, b, dims, preferred_element_type=F32)


def left_dot(x, hot, dims=NN):
    n = x.shape[0]
    out = mm(jnp.concatenate(parts(x), axis=0), hot, dims)
    return out[:n] + out[n:]


def spline_at(row, knot, rows):
    moment = 1.5 + (BLOCK_KNOTS - 3) * (row.astype(F32) + 0.5) / rows
    dist = jnp.abs(moment - knot.astype(F32))
    inner = 2.0 / 3.0 - dist * dist + 0.5 * dist * dist * dist
    rest = 2.0 - dist
    outer = rest * rest * rest / 6.0
    return jnp.where(dist < 1.0, inner, jnp.where(dist < 2.0, outer, 0.0))


def partner(me, i, n):
    if n & (n - 1):
        return lax.rem(me + i, n)
    out, bit = me, 1
    while bit < n:
        out = out + ((i // bit) % 2) * bit * (1 - 2 * ((me // bit) % 2))
        bit *= 2
    return out


def kernel(
    n_sky,
    n_tm,
    observed_in,
    att_partials_in,
    src_partials_in,
    src_slot_in,
    knot_block_in,
    live_count_in,
    sources_in,
    inverses_in,
    attitude_in,
    band_coef_in,
    extra_diag_in,
    band_offsets_in,
    sources_out,
    attitude_out,
    observed,
    att_partials,
    src_partials,
    src_slot,
    knot_block,
    live_count,
    sources,
    inverses,
    attitude,
    band_coef,
    extra_diag,
    band_offsets,
    input_sem,
    knots_all,
    coef_all,
    kb_all,
    slots_all,
    rhs_all,
    grads_all,
    rim_mine,
    rim_all,
    win_mine,
    win_all,
    win_low,
    win_high,
    near_mine,
    edge_all,
    hot_all,
    knots_send,
    knots_recv,
    coef_send,
    coef_recv,
    kb_send,
    kb_recv,
    near_send,
    near_recv,
    pass_send,
    pass_recv,
    slots_send,
    slots_recv,
    rhs_send,
    rhs_recv,
    grads_send,
    grads_recv,
    rim_send,
    rim_recv,
    win_send,
    win_recv,
    far_send,
    low_recv,
    high_recv,
):
    s = lax.axis_index("sky")
    t = lax.axis_index("tm")
    cross, rows = observed.shape
    knots_here = attitude.shape[2]
    blocks = knots_here // BLOCK_KNOTS
    span = blocks + 2 * REACH
    n_blocks = n_sky * blocks
    n_src = sources.shape[1]
    n_band = band_coef.shape[0]
    tile = win_all.shape[2]
    k16 = BLOCK_KNOTS
    per = LANES // blocks
    n_lines = (1 + n_band) * NAX
    n_near = 2 * REACH + 1

    first_t, last_t = t == 0, t == n_tm - 1
    at_low, at_high = s == 0, s == n_sky - 1
    not_first, not_last = t > 0, t < n_tm - 1
    t_up, t_down = jnp.minimum(t + 1, n_tm - 1), jnp.maximum(t - 1, 0)

    barrier = pltpu.get_barrier_semaphore()
    for i in range(n_sky - 1, 0, -1):
        pl.semaphore_signal(barrier, inc=1, device_id=(partner(s, i, n_sky), t), device_id_type=MESH)
    for i in range(n_tm - 1, 0, -1):
        pl.semaphore_signal(barrier, inc=1, device_id=(s, partner(t, i, n_tm)), device_id_type=MESH)

    pairs = (
        (attitude_in, attitude),
        (band_coef_in, band_coef),
        (extra_diag_in, extra_diag),
        (src_slot_in, src_slot),
        (knot_block_in, knot_block),
        (src_partials_in, src_partials),
        (att_partials_in, att_partials),
        (inverses_in, inverses),
        (sources_in, sources),
        (observed_in, observed),
        (live_count_in, live_count),
        (band_offsets_in, band_offsets),
    )
    loads = [
        pltpu.make_async_copy(source, place, input_sem.at[i])
        for i, (source, place) in enumerate(pairs)
    ]
    for load in loads:
        load.start()

    def remote(src, dst, send, recv, to):
        return pltpu.make_async_remote_copy(
            src_ref=src, dst_ref=dst, send_sem=send, recv_sem=recv, device_id=to, device_id_type=MESH
        )

    def to_sky(i):
        return (partner(s, i, n_sky), t)

    def to_tm(i):
        return (s, partner(t, i, n_tm))

    def knots_copy(i):
        return remote(knots_all.at[s], knots_all.at[s], knots_send.at[i], knots_recv.at[i], to_sky(i))

    def coef_copy(i):
        return remote(coef_all.at[s], coef_all.at[s], coef_send.at[i], coef_recv.at[i], to_sky(i))

    def kb_copy(i):
        return remote(kb_all.at[s], kb_all.at[s], kb_send.at[i], kb_recv.at[i], to_sky(i))

    def near_copy(side):
        to = (s, t_up if side == 0 else t_down)
        return remote(near_mine.at[side], edge_all.at[side], near_send.at[side], near_recv.at[side], to)

    def pass_copy(side, i):
        return remote(edge_all.at[side], edge_all.at[side], pass_send.at[side, i], pass_recv.at[side], to_sky(i))

    def slots_copy(i):
        return remote(slots_all.at[t], slots_all.at[t], slots_send.at[i], slots_recv.at[i], to_tm(i))

    def rhs_copy(it, i):
        return remote(rhs_all.at[it, t], rhs_all.at[it, t], rhs_send.at[it, i], rhs_recv.at[it, i], to_tm(i))

    def grads_copy(i):
        return remote(grads_all.at[s], grads_all.at[s], grads_send.at[i], grads_recv.at[i], to_sky(i))

    def rim_copy(side, to_s, slot):
        to = (to_s, t_down if side == 0 else t_up)
        return remote(rim_mine.at[side], rim_all.at[side, slot], rim_send.at[side, to_s], rim_recv.at[side, slot], to)

    def win_copy(i):
        to = to_sky(i)
        return remote(win_mine.at[1 + to[0]], win_all.at[s], win_send.at[i], win_recv.at[i], to)

    def low_copy(slot):
        return remote(win_mine.at[n_sky + 1], win_low.at[slot], far_send.at[0], low_recv.at[slot], (0, t_up))

    def high_copy(slot):
        return remote(win_mine.at[0], win_high.at[slot], far_send.at[1], high_recv.at[slot], (n_sky - 1, t_down))

    for load in loads[:5]:
        load.wait()
    own_knot = iota((k16, knots_here), 0) == iota((k16, knots_here), 1) % k16
    shape = (knots_here, LANES)
    fold = jnp.concatenate(
        [onehot(iota(shape, 1) == iota(shape, 0) // k16 + blocks * c) for c in range(per)], axis=0
    )

    def spread(lines):
        lines = lines + [jnp.zeros((1, knots_here), F32)] * (per - len(lines))
        return jnp.concatenate([jnp.where(own_knot, line, 0.0) for line in lines], axis=1)

    knots_all[s] = left_dot(spread([attitude[a] for a in range(NAX)]), fold)
    slot_row = src_slot[...].astype(F32)
    block_row = knot_block[...].astype(F32)
    slots_all[t] = slot_row
    kb_all[s] = block_row
    bands = [[band_coef[b, a] for a in range(NAX)] for b in range(n_band)]
    inv_diag = []
    for a in range(NAX):
        band_sum = bands[0][a]
        for b in range(1, n_band):
            band_sum = band_sum + bands[b][a]
        inv_diag.append(1.0 / (extra_diag[a] + 2.0 * band_sum))
    lines = inv_diag + [bands[b][a] * inv_diag[a] for b in range(n_band) for a in range(NAX)]
    coef = left_dot(
        jnp.concatenate([spread(lines[c : c + per]) for c in range(0, n_lines, per)], axis=0), fold
    )
    coef_all[s] = coef
    edge_lane = iota((k16, LANES), 1) // REACH
    for side in range(2):
        edge = jnp.zeros((k16, LANES), F32)
        for l in range(n_lines):
            j, c = l // per, l % per
            begin = c * blocks + (blocks - REACH if side == 0 else 0)
            moved = pltpu.roll(coef[j * k16 : (j + 1) * k16], (REACH * l - begin) % LANES, 1)
            edge = jnp.where(edge_lane == l, moved, edge)
        near_mine[side] = edge

    pl.semaphore_wait(barrier, (n_sky - 1) + (n_tm - 1))
    for i in range(n_sky - 1, 0, -1):
        knots_copy(i).start()
    for i in range(n_tm - 1, 0, -1):
        slots_copy(i).start()
    take_low, take_high = jnp.logical_and(at_high, not_first), jnp.logical_and(at_low, not_last)

    @pl.when(jnp.logical_and(at_high, not_last))
    def _():
        near_copy(0).start()

    @pl.when(jnp.logical_and(at_low, not_first))
    def _():
        near_copy(1).start()

    for i in range(n_sky - 1, 0, -1):
        kb_copy(i).start()
    for i in range(n_sky - 1, 0, -1):
        coef_copy(i).start()

    for load in loads[5:]:
        load.wait()
    lane = iota((1, cross), 1)
    live = lane < live_count[0]

    shape = (n_src, cross)
    src_hot = onehot(iota(shape, 0).astype(F32) == slot_row)
    gap_rows = jnp.zeros((8 - NPAR, n_src), F32)
    src_list = [x for q in range(NPAR) for x in (inverses[q], gap_rows)]
    gathered = left_dot(jnp.concatenate(src_list + [sources[...], gap_rows], axis=0), src_hot)

    eye = onehot(iota((rows, rows), 0) == iota((rows, rows), 1))
    par = [mm(eye, src_partials[p], NT) for p in range(NPAR)]
    att = [mm(eye, att_partials[a], NT) for a in range(NAX)]

    def source_term(values):
        total = par[0] * values[0:1]
        for p in range(1, NPAR):
            total = total + par[p] * values[p : p + 1]
        return total

    base = jnp.transpose(observed[...]) - source_term(gathered[NPAR * 8 :])

    shape = (k16, 2 * rows)
    high, low = parts(spline_at(iota(shape, 1) % rows, iota(shape, 0), rows))
    low = jnp.where(iota(shape, 1) < rows, low.astype(F32), 0.0).astype(BF16)
    back = jnp.concatenate([high, low], axis=0)
    shape = (rows, 3 * k16)
    high, low = parts(spline_at(iota(shape, 0), iota(shape, 1) % k16, rows))
    look = jnp.where(iota(shape, 1) < 2 * k16, high.astype(F32), low.astype(F32)).astype(BF16)

    def back_dot(value):
        spread = jnp.concatenate([x * value for x in att], axis=1)
        out = mm(back, jnp.concatenate(parts(spread), axis=0))
        return out[:k16] + out[k16:]

    def look_dot(knots):
        high, low = parts(knots)
        return mm(look, jnp.concatenate([high, low, high], axis=0))

    cross_terms = [back_dot(par[q]) for q in range(NPAR)]

    def against_params(value):
        return jnp.concatenate(
            [jnp.sum(par[p] * value, axis=0, keepdims=True) for p in range(NPAR)]
            + [jnp.zeros((8 - NPAR, cross), F32)],
            axis=0,
        )

    on_base = against_params(base)

    near_row = jnp.concatenate([block_row + (m - REACH) for m in range(n_near)], axis=1)
    shape = (n_sky * LANES, n_near * cross)
    found = iota((n_sky * LANES, 1), 0)
    found = found // LANES * blocks + found % blocks
    near_hot = onehot(found.astype(F32) == near_row)
    found = iota((LANES, 1), 0) % REACH
    low_hot = onehot((found - REACH).astype(F32) == near_row)
    high_hot = onehot((found + n_blocks).astype(F32) == near_row)
    near_hot = jnp.concatenate([near_hot, low_hot, high_hot], axis=0)
    mid = slice(REACH * cross, (REACH + 1) * cross)

    def window_col(count, first):
        m = iota((count * tile, LANES), 0)
        h, at = m // tile + first, m % tile
        i = at
        for a in range(1, NAX):
            i = i - jnp.where(at >= a * span, span, 0)
        return jnp.where(at >= NAX * span, -1, h * blocks - REACH + i).astype(F32)

    line_lane = iota((k16, n_sky * LANES), 1) % LANES // blocks

    def lanes_of(tiles):
        return jnp.concatenate([tiles[:, a * cross : (a + 1) * cross] for a in range(NAX)], axis=0)

    def rows_of(lines):
        return jnp.concatenate([lines[a * k16 : (a + 1) * k16] for a in range(NAX)], axis=1)

    def pick_axes(lines, count):
        lane = iota((k16, count * tile), 1) % tile
        picked = lines[(NAX - 1) * k16 :]
        for a in range(NAX - 2, -1, -1):
            picked = jnp.where(lane < (a + 1) * span, lines[a * k16 : (a + 1) * k16], picked)
        return picked

    for i in range(1, n_tm):
        slots_copy(i).wait_recv()
    slots_row = jnp.concatenate([slots_all[i] for i in range(n_tm)], axis=1)
    slot_col = jnp.transpose(jnp.broadcast_to(slot_row, (LANES, cross)))[:, :1]
    same_source = onehot(slot_col == slots_row)

    @pl.when(take_low)
    def _():
        near_copy(0).wait_recv()
        for i in range(n_sky - 1, 0, -1):
            pass_copy(0, i).start()

    @pl.when(take_high)
    def _():
        near_copy(1).wait_recv()
        for i in range(n_sky - 1, 0, -1):
            pass_copy(1, i).start()

    def shift_rows(outs, ins):
        shape = (outs * n_band * k16, ins * k16)
        c, d = iota(shape, 0), iota(shape, 1)
        m, b = c // (n_band * k16), c // k16 % n_band
        gap = jnp.abs(d - (m + (ins - outs) // 2) * k16 - c % k16)
        offset = jnp.zeros(shape, jnp.int32)
        for i in range(n_band):
            offset = jnp.where(b == i, band_offsets[i], offset)
        hot = onehot(gap == offset)
        return jnp.concatenate([hot, hot], axis=1)

    shifts = [shift_rows(n_near - 2 * i, n_near - 2 * i + 2) for i in range(1, SWEEPS)]

    def back_rows(outs, ins):
        shape = (ins * k16, outs * n_band * k16)
        c, d = iota(shape, 0), iota(shape, 1)
        m, b = d // (n_band * k16), d // k16 % n_band
        gap = jnp.abs(c - (m + (ins - outs) // 2) * k16 - d % k16)
        offset = jnp.zeros(shape, jnp.int32)
        for i in range(n_band):
            offset = jnp.where(b == i, band_offsets[i], offset)
        hot = onehot(gap == offset)
        return jnp.concatenate([hot, hot], axis=1)

    shifts_back = [back_rows(n_near - 2 * i, n_near - 2 * i + 2) for i in range(1, SWEEPS)]

    def smooth_back(value, inv, terms):
        total = [None] * n_near
        total[REACH] = value
        slots = [value]
        for i in range(SWEEPS - 1, 0, -1):
            spread = [
                terms[b][m + i - 1] * slots[m] for m in range(n_near - 2 * i) for b in range(n_band)
            ]
            out = mm(shifts_back[i - 1], jnp.concatenate(parts(jnp.concatenate(spread, axis=0)), axis=0))
            slots = [out[m * k16 : (m + 1) * k16] for m in range(n_near - 2 * i + 2)]
            for m, slot in enumerate(slots):
                at = m + i - 1
                total[at] = slot if total[at] is None else total[at] + slot
        return [inv[m] * total[m] for m in range(n_near)]

    def smooth_near(first, terms):
        delta = first
        for i in range(1, SWEEPS):
            sums = mm(shifts[i - 1], jnp.concatenate(parts(jnp.concatenate(delta, axis=0)), axis=0))
            delta = []
            for m in range(n_near - 2 * i):
                at = m + i
                total = first[at]
                for b in range(n_band):
                    row = (m * n_band + b) * k16
                    total = total + terms[b][at - 1] * sums[row : row + k16]
                delta.append(total)
        return delta[0]

    def smooth(grad, inv, terms):
        first = grad * inv
        delta = first
        for sweep in range(SWEEPS - 1):
            near = jnp.concatenate([pltpu.roll(delta, 1, 1), delta, pltpu.roll(delta, tile - 1, 1)], axis=0)
            sums = mm(shifts[-1], jnp.concatenate(parts(near), axis=0))
            delta = first
            for b in range(n_band):
                delta = delta + terms[b] * sums[b * k16 : (b + 1) * k16]
        return delta

    for i in range(1, n_sky):
        knots_copy(i).wait_recv()
    knots = jnp.concatenate([knots_all[h] for h in range(n_sky)], axis=1)
    knots = jnp.concatenate([jnp.where(line_lane == a, knots, 0.0) for a in range(NAX)], axis=0)
    fetched = rows_of(left_dot(knots, near_hot[: n_sky * LANES, mid]))

    def rhs_term(fetched):
        out = []
        for q in range(NPAR):
            term = jnp.sum(fetched * cross_terms[q], axis=0, keepdims=True)
            total = term[:, :cross]
            for a in range(1, NAX):
                total = total + term[:, a * cross : (a + 1) * cross]
            out.append(total)
        out.append(jnp.zeros((8 - NPAR, cross), F32))
        return jnp.concatenate(out, axis=0)

    def send_rhs(it, rhs):
        rhs_all[it, t] = jnp.where(live, rhs, 0.0)
        for i in range(n_tm - 1, 0, -1):
            rhs_copy(it, i).start()

    def grads_of(base, fetched):
        seen = look_dot(fetched)
        resid = base
        for a in range(NAX):
            resid = resid - att[a] * seen[:, a * cross : (a + 1) * cross]
        return back_dot(jnp.where(live, resid, 0.0))

    def wait_rhs(it):
        for i in range(1, n_tm):
            rhs_copy(it, i).wait_recv()
        return jnp.concatenate([rhs_all[it, i] for i in range(n_tm)], axis=1)

    live_all = jnp.concatenate([live] * NAX, axis=1)

    def step_of(rhs):
        normal = left_dot(rhs, same_source, NT)
        return [
            jnp.sum(gathered[q * 8 : (q + 1) * 8] * normal, axis=0, keepdims=True)
            for q in range(NPAR)
        ]

    def move_grads(grads, step):
        total = jnp.concatenate([step[0]] * NAX, axis=1) * cross_terms[0]
        for q in range(1, NPAR):
            total = total + jnp.concatenate([step[q]] * NAX, axis=1) * cross_terms[q]
        return grads - jnp.where(live_all, total, 0.0)

    send_rhs(0, on_base - rhs_term(fetched))
    grads = grads_of(base, fetched)

    for i in range(1, n_sky):
        kb_copy(i).wait_recv()

    prebuilt = hot_all.shape[0] == n_sky

    block_col = jnp.transpose(jnp.broadcast_to(block_row, (LANES, cross)))
    near_col = jnp.concatenate([block_col + (m - REACH) for m in range(n_near)], axis=0)

    def sender_hot(h):
        return onehot(near_col == kb_all[h])

    if prebuilt:
        for h in range(n_sky):
            hot_all[h] = sender_hot(h)

    rim_row = iota((k16, cross), 0)
    rim_block = jnp.where(rim_row < 8, rim_row, n_blocks - REACH - 8 + rim_row)
    rim_hot = onehot(
        jnp.logical_and(rim_row % 8 < REACH, rim_block.astype(F32) == block_row)
    )

    rhs = wait_rhs(0)
    rhs_total = rhs
    step = step_of(rhs)
    grads = move_grads(grads, step)
    grads_all[s] = grads
    for i in range(n_sky - 1, n_sky // 2 - 1, -1):
        grads_copy(i).start()

    high, low = parts(lanes_of(grads))
    gap_rows = jnp.zeros((LANES - NAX * k16, cross), BF16)
    rims = mm(rim_hot, jnp.concatenate([high, gap_rows], axis=0), NT) + mm(
        rim_hot, jnp.concatenate([low, gap_rows], axis=0), NT
    )
    rim_mine[0] = rims[:REACH]
    rim_mine[1] = rims[8 : 8 + REACH]

    @pl.when(not_first)
    def _():
        for i in range(n_sky - 1, -1, -1):
            rim_copy(0, partner(s, i, n_sky), s).start()

    @pl.when(not_last)
    def _():
        for i in range(n_sky - 1, -1, -1):
            rim_copy(1, partner(s, i, n_sky), s).start()

    for i in range(n_sky // 2 - 1, 0, -1):
        grads_copy(i).start()

    base = base - source_term(jnp.concatenate(step, axis=0))
    on_base = against_params(base) - rhs_term(fetched)
    for i in range(1, n_sky):
        coef_copy(i).wait_recv()

    @pl.when(jnp.logical_and(not_first, jnp.logical_not(at_high)))
    def _():
        pass_copy(0, 1).wait_recv()

    @pl.when(jnp.logical_and(not_last, jnp.logical_not(at_low)))
    def _():
        pass_copy(1, 1).wait_recv()

    @pl.when(first_t)
    def _():
        edge_all[0] = jnp.zeros(edge_all.shape[1:], F32)
        rim_all[1] = jnp.zeros(rim_all.shape[1:], F32)

    @pl.when(last_t)
    def _():
        edge_all[1] = jnp.zeros(edge_all.shape[1:], F32)
        rim_all[0] = jnp.zeros(rim_all.shape[1:], F32)

    def coef_lines(first, last):
        out = []
        for l in range(first, last):
            j, c = l // per, l % per
            line = jnp.concatenate([coef_all[h, j * k16 : (j + 1) * k16] for h in range(n_sky)], axis=1)
            ends = [jnp.where(edge_lane == l, edge_all[side], 0.0) for side in range(2)]
            out.append(jnp.concatenate([jnp.where(line_lane == c, line, 0.0)] + ends, axis=1))
        return jnp.concatenate(out, axis=0)

    inv_lines, term_lines = coef_lines(0, NAX), coef_lines(NAX, n_lines)
    inv_near = left_dot(inv_lines, near_hot)
    got = left_dot(term_lines, near_hot[:, cross : (n_near - 1) * cross])
    terms_near = [
        [
            rows_of(got[b * NAX * k16 : (b + 1) * NAX * k16, m * cross : (m + 1) * cross])
            for m in range(n_near - 2)
        ]
        for b in range(n_band)
    ]

    inv_slots = [rows_of(inv_near[:, m * cross : (m + 1) * cross]) for m in range(n_near)]
    weights = smooth_back(
        jnp.concatenate(cross_terms, axis=1),
        [jnp.concatenate([x] * NPAR, axis=1) for x in inv_slots],
        [[jnp.concatenate([x] * NPAR, axis=1) for x in row] for row in terms_near],
    )

    shape = (2 * REACH * LANES, 2 * tile)
    c, d = iota(shape, 0), iota(shape, 1)
    r, c = c // LANES, c % LANES
    spot = (c // k16) * span + jnp.where(r < REACH, r, tile + blocks + r)
    rim_fold = onehot(jnp.logical_and(c < NAX * k16, d == spot))
    rim_knot = iota((k16, LANES), 0) == iota((k16, LANES), 1) % k16

    group = 2 if n_sky % 2 == 0 else 1

    def scatter(j, total):
        home = partner(s // group, j, n_sky // group) * group
        lines = jnp.concatenate([lanes_of(grads_all[home + x]) for x in range(group)], axis=1)
        hots = [hot_all[home + x] if prebuilt else sender_hot(home + x) for x in range(group)]
        return total + left_dot(lines, jnp.concatenate(hots, axis=1), NT)

    for x in range(1, group):
        grads_copy(x).wait_recv()
    grad = scatter(0, jnp.zeros((NAX * k16, n_near * cross), F32))

    def add_group(j, total):
        for x in range(group):
            grads_copy(j * group + x).wait_recv()
        return scatter(j, total)

    if prebuilt:
        for j in range(1, n_sky // group - 1):
            grad = add_group(j, grad)
    else:
        grad = lax.fori_loop(1, n_sky // group - 1, add_group, grad)

    @pl.when(not_last)
    def _():
        for i in range(n_sky):
            rim_copy(0, i, i).wait_recv()

    @pl.when(not_first)
    def _():
        for i in range(n_sky):
            rim_copy(1, i, i).wait_recv()

    rim_rows = []
    for side in (1, 0):
        total = rim_all[side, 0]
        for i in range(1, n_sky):
            total = total + rim_all[side, i]
        rim_rows = rim_rows + [total[i : i + 1] for i in range(REACH)]
    rim_cols = jnp.transpose(
        jnp.concatenate(rim_rows + [jnp.zeros((LANES - 2 * REACH, LANES), F32)], axis=0)
    )
    found = iota((LANES, 1), 0)
    found = jnp.where(found < REACH, found - REACH, found + n_blocks - REACH)
    found = jnp.where(iota((LANES, 1), 0) < 2 * REACH, found, -8 * REACH)
    grad = grad + left_dot(rim_cols[: NAX * k16], onehot(found.astype(F32) == near_row))

    grad = add_group(n_sky // group - 1, grad)


    slots = [rows_of(grad[:, m * cross : (m + 1) * cross]) for m in range(n_near)]
    out = []
    for q in range(NPAR):
        total = None
        for a in range(NAX):
            at = (q * NAX + a) * cross
            for m in range(n_near):
                term = weights[m][:, at : at + cross] * slots[m][:, a * cross : (a + 1) * cross]
                total = term if total is None else total + term
        out.append(jnp.sum(total, axis=0, keepdims=True))
    out.append(jnp.zeros((8 - NPAR, cross), F32))
    send_rhs(1, on_base - jnp.concatenate(out, axis=0))
    fetched = fetched + smooth_near([slots[m] * inv_slots[m] for m in range(n_near)], terms_near)
    grads = grads_of(base, fetched)
    win_hot = onehot(window_col(n_sky + 2, -1) == block_row)
    own_col = window_col(1, s)
    own_row = jnp.concatenate([kb_all[h] for h in range(n_sky)], axis=1)
    own_hot = onehot(jnp.concatenate([own_col] * n_sky, axis=1) == own_row)
    lines = jnp.concatenate([lanes_of(grads_all[h]) for h in range(n_sky)], axis=1)
    grad_own = pick_axes(left_dot(lines, own_hot, NT), 1)
    rim_tiles = left_dot(
        jnp.concatenate([jnp.where(rim_knot, row, 0.0) for row in rim_rows], axis=1), rim_fold
    )
    grad_own = grad_own + jnp.where(at_low, rim_tiles[:, :tile], 0.0)
    grad_own = grad_own + jnp.where(at_high, rim_tiles[:, tile:], 0.0)
    rhs = wait_rhs(1)
    rhs_total = rhs_total + rhs
    grads = move_grads(grads, step_of(rhs))
    picked = pick_axes(left_dot(lanes_of(grads), win_hot, NT), n_sky + 2)
    for h in range(n_sky + 2):
        win_mine[h] = picked[:, h * tile : (h + 1) * tile]

    for i in range(n_sky - 1, 0, -1):
        win_copy(i).start()

    @pl.when(not_last)
    def _():
        low_copy(s).start()

    @pl.when(not_first)
    def _():
        high_copy(s).start()

    win_all[s] = win_mine[1 + s]
    from_low, from_high = jnp.logical_and(at_low, not_first), jnp.logical_and(at_high, not_last)

    @pl.when(jnp.logical_not(from_low))
    def _():
        win_low[...] = jnp.zeros(win_low.shape, F32)

    @pl.when(jnp.logical_not(from_high))
    def _():
        win_high[...] = jnp.zeros(win_high.shape, F32)

    full_hot = onehot(iota((n_src, n_tm * cross), 0).astype(F32) == slots_row)
    normal_all = left_dot(rhs_total, full_hot, NT)[:NPAR]
    steps = [jnp.sum(inverses[q] * normal_all, axis=0, keepdims=True) for q in range(NPAR)]
    sources_out[...] = sources[...] + jnp.concatenate(steps, axis=0)
    shape = (n_sky * LANES, tile)
    m, at = iota((n_sky * LANES, 1), 0), iota((1, tile), 1)
    i = at
    for a in range(1, NAX):
        i = i - jnp.where(at >= a * span, span, 0)
    own_place = jnp.where(at >= NAX * span, -8 * REACH, s * blocks - REACH + i).astype(F32)
    found = [
        m // LANES * blocks + m % blocks,
        iota((LANES, 1), 0) % REACH - REACH,
        iota((LANES, 1), 0) % REACH + n_blocks,
    ]
    coef_hot = jnp.concatenate([onehot(x.astype(F32) == own_place) for x in found], axis=0)
    got = left_dot(jnp.concatenate([inv_lines, term_lines], axis=0), coef_hot)
    own = [pick_axes(got[b * NAX * k16 : (b + 1) * NAX * k16], 1) for b in range(n_band + 1)]
    inv_own, terms_own = own[0], own[1:]
    shape = (knots_here, tile)
    unfold = jnp.concatenate(
        [onehot(iota(shape, 1) == (iota(shape, 0) // k16) + (span * a + REACH)) for a in range(NAX)], axis=0
    )

    for i in range(1, n_sky):
        knots_copy(i).wait_send()
        coef_copy(i).wait_send()
        kb_copy(i).wait_send()
        grads_copy(i).wait_send()
    for i in range(1, n_tm):
        slots_copy(i).wait_send()
        for it in range(ITERS):
            rhs_copy(it, i).wait_send()

    @pl.when(jnp.logical_and(at_high, not_last))
    def _():
        near_copy(0).wait_send()

    @pl.when(jnp.logical_and(at_low, not_first))
    def _():
        near_copy(1).wait_send()

    @pl.when(take_low)
    def _():
        for i in range(1, n_sky):
            pass_copy(0, i).wait_send()

    @pl.when(take_high)
    def _():
        for i in range(1, n_sky):
            pass_copy(1, i).wait_send()

    @pl.when(not_first)
    def _():
        for i in range(n_sky):
            rim_copy(0, i, s).wait_send()

    @pl.when(not_last)
    def _():
        for i in range(n_sky):
            rim_copy(1, i, s).wait_send()

    for i in range(1, n_sky):
        win_copy(i).wait_recv()

    @pl.when(from_low)
    def _():
        for i in range(n_sky):
            low_copy(i).wait_recv()

    @pl.when(from_high)
    def _():
        for i in range(n_sky):
            high_copy(i).wait_recv()

    grad = grad_own
    for i in range(n_sky):
        grad = grad + (win_all[i] + win_low[i] + win_high[i])
    moved = smooth(grad, inv_own, terms_own)

    line = left_dot(moved, unfold, NT)
    for a in range(NAX):
        own = jnp.where(own_knot, line[:, a * knots_here : (a + 1) * knots_here], 0.0)
        attitude_out[a] = attitude[a] + jnp.sum(own, axis=0, keepdims=True)

    for i in range(1, n_sky):
        win_copy(i).wait_send()

    @pl.when(not_first)
    def _():
        high_copy(s).wait_send()

    @pl.when(not_last)
    def _():
        low_copy(s).wait_send()


def finish(sources_in, attitude_in, sources_out, attitude_out, sem):
    copies = [
        pltpu.make_async_copy(sources_in, sources_out, sem.at[0]),
        pltpu.make_async_copy(attitude_in, attitude_out, sem.at[1]),
    ]
    for copy in copies:
        copy.start()
    for copy in copies:
        copy.wait()


def per_device(
    observed,
    att_partials,
    src_partials,
    src_slot,
    knot_block,
    live_count,
    sources,
    inverses,
    attitude,
    band_coef,
    extra_diag,
    band_offsets,
):
    n_sky, n_tm = lax.axis_size("sky"), lax.axis_size("tm")
    blocks = attitude.shape[2] // BLOCK_KNOTS
    cross = src_slot.shape[0]
    k16 = BLOCK_KNOTS
    tile = -(-NAX * (blocks + 2 * REACH) // LANES) * LANES
    n_tiles = -(-(1 + band_coef.shape[0]) * NAX * blocks // LANES)
    n_near = (2 * REACH + 1) * cross
    n_hot = n_sky if n_sky * n_near * cross * 2 <= HOT_CAP else 1
    vmem = pl.BlockSpec(memory_space=pltpu.VMEM)
    hbm = pl.BlockSpec(memory_space=pl.ANY)
    dma = pltpu.SemaphoreType.DMA
    results = pl.pallas_call(
        functools.partial(kernel, n_sky, n_tm),
        out_shape=(
            pltpu.VMEM(sources.shape, F32),
            pltpu.VMEM(attitude.shape, F32),
        ),
        in_specs=[hbm] * 12,
        out_specs=(vmem, vmem),
        scratch_shapes=[
            pltpu.VMEM(observed.shape, F32),
            pltpu.VMEM(att_partials.shape, BF16),
            pltpu.VMEM(src_partials.shape, BF16),
            pltpu.VMEM((1, cross), jnp.int32),
            pltpu.VMEM((1, cross), jnp.int32),
            pltpu.SMEM(live_count.shape, jnp.int32),
            pltpu.VMEM(sources.shape, F32),
            pltpu.VMEM(inverses.shape, F32),
            pltpu.VMEM(attitude.shape, F32),
            pltpu.VMEM(band_coef.shape, F32),
            pltpu.VMEM(extra_diag.shape, F32),
            pltpu.SMEM(band_offsets.shape, jnp.int32),
            dma((12,)),
            pltpu.VMEM((n_sky, k16, LANES), F32),
            pltpu.VMEM((n_sky, n_tiles * k16, LANES), F32),
            pltpu.VMEM((n_sky, 1, cross), F32),
            pltpu.VMEM((n_tm, 1, cross), F32),
            pltpu.VMEM((ITERS, n_tm, 8, cross), F32),
            pltpu.VMEM((n_sky, k16, NAX * cross), F32),
            pltpu.VMEM((2, REACH, LANES), F32),
            pltpu.VMEM((2, n_sky, REACH, LANES), F32),
            pltpu.VMEM((n_sky + 2, k16, tile), F32),
            pltpu.VMEM((n_sky, k16, tile), F32),
            pltpu.VMEM((n_sky, k16, tile), F32),
            pltpu.VMEM((n_sky, k16, tile), F32),
            pltpu.VMEM((2, k16, LANES), F32),
            pltpu.VMEM((2, k16, LANES), F32),
            pltpu.VMEM((n_hot, n_near, cross), BF16),
            dma((n_sky,)),
            dma((n_sky,)),
            dma((n_sky,)),
            dma((n_sky,)),
            dma((n_sky,)),
            dma((n_sky,)),
            dma((2,)),
            dma((2,)),
            dma((2, n_sky)),
            dma((2,)),
            dma((n_tm,)),
            dma((n_tm,)),
            dma((ITERS, n_tm)),
            dma((ITERS, n_tm)),
            dma((n_sky,)),
            dma((n_sky,)),
            dma((2, n_sky)),
            dma((2, n_sky)),
            dma((n_sky,)),
            dma((n_sky,)),
            dma((2,)),
            dma((n_sky,)),
            dma((n_sky,)),
        ],
        compiler_params=pltpu.CompilerParams(
            collective_id=0, has_side_effects=True, vmem_limit_bytes=VMEM_LIMIT
        ),
    )(
        observed,
        att_partials,
        src_partials,
        src_slot[None, :],
        knot_block[None, :],
        live_count,
        sources,
        inverses,
        attitude,
        band_coef,
        extra_diag,
        band_offsets,
    )
    return pl.pallas_call(
        finish,
        out_shape=(
            jax.ShapeDtypeStruct(sources.shape, F32),
            jax.ShapeDtypeStruct(attitude.shape, F32),
        ),
        in_specs=[vmem] * 2,
        out_specs=(hbm, hbm),
        scratch_shapes=[dma((2,))],
        compiler_params=pltpu.CompilerParams(vmem_limit_bytes=1 << 20),
    )(*results)


def solution(mesh):
    placed = (
        P(("sky", "tm"), None),
        P(None, ("sky", "tm"), None),
        P(None, ("sky", "tm"), None),
        P(("sky", "tm")),
        P(("sky", "tm")),
        P(("sky", "tm")),
        P(None, "sky"),
        P(None, None, "sky"),
        P(None, "tm", "sky"),
        P(None, None, "tm", "sky"),
        P(None, "tm", "sky"),
        P(),
    )
    return jax.shard_map(
        per_device,
        mesh=mesh,
        in_specs=placed,
        out_specs=(P(None, "sky"), P(None, "tm", "sky")),
        check_vma=False,
    )
```
